32 devices in a mesh: sec: 8 (over z, y), tile: 4 (over x, core).
Axes of the slice: x: 2, y: 2, z: 4, core: 2. Of those that a mesh axis runs over, the one named last changes fastest.
Arguments:
- patches: bfloat16 [48, 8, 8, 128, 128], P('sec', 'tile'), may hold values from -6 to 6
- pair_flags: int32 [48, 3], P('sec'), may hold values 0 or 1
- nodes: float32 [2, 48, 8, 8], P(None, 'sec', 'tile'), may hold values from -6 to 6
Outputs:
- relaxed: float32 [2, 48, 8, 8], P(None, 'sec', 'tile')
- measured: float32 [2, 48, 3, 8, 8], P(None, 'sec', None, 'tile')
The draws below stay inside these ranges and needn't reach their ends.
Inputs may be any that keep to these rules, and one draw needn't show every extreme that they name: `pair_flags`: flags of pairs whose partner lies past the last section are ignored.
All inputs are finite; a program needn't handle non-finite values. No bound on the sum of `pair_flags` on one device may be relied on, other than what follows from the above.
Results may differ from the reference program's by a relative error of at most 0.0081.
Values may be sent and summed in bfloat16 or wider, within the bound.
A program may use at most 128 MiB of HBM per device.

```python
import math
import jax
import jax.numpy as jnp
from jax import lax

P_SIZE = 128
COLS = 8
OFFS = 3
SWEEPS = 8
SECTIONS = 48
ROWS = 8


def place_ends(drawn, rng, smallest, high):
    index_at = [jax.random.randint(jax.random.fold_in(rng, axis), (), 0, length) for axis, length in enumerate(drawn.shape)]
    longest = drawn.shape.index(max(drawn.shape))
    next_to = index_at[:longest] + [(index_at[longest] + 1) % drawn.shape[longest]] + index_at[longest + 1:]
    return drawn.at[tuple(index_at)].set(smallest).at[tuple(next_to)].set(high)


def steps_of(rng, shape, split, low, high):
    factor_of = 1.0
    for position, shards_of in split:
        heights = jax.random.uniform(jax.random.fold_in(jax.random.fold_in(rng, 6), position), (shards_of,), jnp.float32, low / len(split), high / len(split))
        factor_of = factor_of * jnp.repeat(jnp.exp(heights), shape[position] // shards_of).reshape((-1,) + (1,) * (len(shape) - 1 - position))
    return factor_of


def centred(own_key, dims, width, most, split=(), held_as=jnp.bfloat16):
    gain = steps_of(own_key, dims, split, -0.22, 0.18) if split else 1.0
    entries = jax.random.normal(own_key, dims, jnp.float32) * width * gain
    return jnp.minimum(jnp.maximum(entries, -most), most).astype(held_as)


def setup_inputs(seed: int = 0) -> dict:
    streams_of = jax.random.split(jax.random.key(seed), 4)
    patches = centred(streams_of[0], (SECTIONS, ROWS, COLS, P_SIZE, P_SIZE), 1.0, 6.0, ((0, 8), (1, 4)))
    pair_flags = place_ends((jax.random.randint(streams_of[1], (SECTIONS, OFFS), 0, 3) < 2).astype(jnp.int32), jax.random.fold_in(streams_of[1], 1), 0, 1)
    nodes = centred(streams_of[2], (2, SECTIONS, ROWS, COLS), 1.0, 6.0, ((1, 8), (2, 4)), jnp.float32)
    return {"patches": patches, "pair_flags": pair_flags, "nodes": nodes}


STEP_SIZE = 0.08
EPSILON = 1e-6


def transform_tables(length):
    index = jnp.arange(length, dtype=jnp.int32)
    phase = ((index[:, None] * index[None, :]) % length).astype(jnp.float32) * (2.0 * math.pi / length)
    cosine = jnp.cos(phase)
    sine = jnp.sin(phase)
    forward_first = jnp.concatenate([cosine, sine], axis=1).astype(jnp.bfloat16)
    forward_second = jnp.stack([jnp.stack([cosine, -sine], 1), jnp.stack([-sine, -cosine], 1)], 0).astype(jnp.bfloat16)
    inverse_first = jnp.stack([jnp.stack([cosine, sine], 1), jnp.stack([-sine, cosine], 1)], 0).astype(jnp.bfloat16)
    inverse_second = jnp.stack([cosine, -sine], 1).astype(jnp.bfloat16)
    shifts = jnp.where(index < length // 2, index, index - length).astype(jnp.float32)
    return forward_first, forward_second, inverse_first, inverse_second, shifts


def spectrum(block, tabs):
    length = block.shape[-1]
    half = jnp.einsum("...aj,jm->...am", block.astype(jnp.float32), tabs[0].astype(jnp.float32)).astype(jnp.bfloat16)
    half = half.reshape(half.shape[:-1] + (2, length))
    return jnp.einsum("rahj,...jhk->...rak", tabs[1].astype(jnp.float32), half.astype(jnp.float32)).astype(jnp.bfloat16)


def measure(first_spec, second_spec, weight, tabs):
    length = first_spec.shape[-1]
    left = first_spec.astype(jnp.float32)
    right = second_spec.astype(jnp.float32)
    real = left[..., 0, :, :] * right[..., 0, :, :] + left[..., 1, :, :] * right[..., 1, :, :]
    imag = left[..., 0, :, :] * right[..., 1, :, :] - left[..., 1, :, :] * right[..., 0, :, :]
    cross = jnp.stack([real, imag], axis=-3).astype(jnp.bfloat16)
    back = jnp.einsum("...qaj,qjrk->...rak", cross.astype(jnp.float32), tabs[2].astype(jnp.float32)).astype(jnp.bfloat16)
    corr = jnp.einsum("arj,...rjk->...ak", tabs[3].astype(jnp.float32), back.astype(jnp.float32)) * (1.0 / float(length) ** 3)
    power = corr * corr
    total = jnp.mean(power, axis=(-2, -1)) + EPSILON
    along_rows = jnp.mean(power * tabs[4][:, None], axis=(-2, -1))
    along_cols = jnp.mean(power * tabs[4][None, :], axis=(-2, -1))
    return jnp.stack([along_rows / total, along_cols / total], 0) * weight


def plane_force(u):
    rows = u.shape[2]
    cols = u.shape[3]
    row_place = jnp.arange(rows, dtype=jnp.int32)
    col_place = jnp.arange(cols, dtype=jnp.int32)
    has_up = (row_place > 0).astype(jnp.float32)[:, None]
    has_down = (row_place < rows - 1).astype(jnp.float32)[:, None]
    has_left = (col_place > 0).astype(jnp.float32)[None, :]
    has_right = (col_place < cols - 1).astype(jnp.float32)[None, :]
    zero_row = jnp.zeros_like(u[:, :, :1])
    zero_col = jnp.zeros_like(u[..., :1])
    above = jnp.concatenate([zero_row, u[:, :, :-1]], axis=2)
    below = jnp.concatenate([u[:, :, 1:], zero_row], axis=2)
    left = jnp.concatenate([zero_col, u[..., :-1]], axis=3)
    right = jnp.concatenate([u[..., 1:], zero_col], axis=3)
    return has_up * (above - u) + has_down * (below - u) + has_left * (left - u) + has_right * (right - u)


def reference(patches, pair_flags, nodes):
    tabs = transform_tables(P_SIZE)
    spectra = lax.map(lambda block: spectrum(block, tabs), patches)
    sections = patches.shape[0]
    offsets = jnp.arange(1, OFFS + 1, dtype=jnp.int32)
    placed = jnp.arange(sections, dtype=jnp.int32)
    weights = pair_flags.astype(jnp.float32) * ((placed[:, None] + offsets[None, :]) < sections).astype(jnp.float32)

    def per_section(index):
        own = lax.dynamic_index_in_dim(spectra, index, 0, keepdims=False)
        results = []
        for step in range(OFFS):
            where = jnp.minimum(index + step + 1, sections - 1).astype(jnp.int32)
            other = lax.dynamic_index_in_dim(spectra, where, 0, keepdims=False)
            results.append(measure(own, other, weights[index, step], tabs))
        return jnp.stack(results, axis=1)

    measured = lax.map(per_section, placed)
    measured = jnp.transpose(measured, (1, 0, 2, 3, 4))
    u = nodes
    for sweep in range(SWEEPS):
        spring = jnp.zeros_like(u)
        for step in range(OFFS):
            offset = step + 1
            ahead = jnp.concatenate([u[:, offset:], jnp.zeros_like(u[:, :offset])], axis=1)
            resid = weights[None, :, step, None, None] * (ahead - u - measured[:, :, step])
            spring = spring + resid - jnp.concatenate([jnp.zeros_like(resid[:, :offset]), resid[:, :sections - offset]], axis=1)
        u = u + STEP_SIZE * (plane_force(u) + spring)
    return u, measured
```

```python
import functools
import math

import jax
import jax.numpy as jnp
import numpy as np
from jax import lax
from jax.experimental import pallas as pl
from jax.experimental.pallas import tpu as pltpu
from jax.sharding import PartitionSpec as P

SWEEPS = 8
STEP_SIZE = 0.08
EPSILON = 1e-06
LANES = 128
TILE = 8
MESH = pl.DeviceIdType.MESH


def tables(n):
    h = n // 2
    k = np.arange(n)
    phase = (k[:, None] * k[None, :] % n) * (2.0 * math.pi / n)
    c = np.asarray(np.cos(phase), np.float32).astype(jnp.bfloat16).astype(np.float32)
    s = np.asarray(np.sin(phase), np.float32).astype(jnp.bfloat16).astype(np.float32)
    part = h + TILE
    first = np.zeros((2 * part, 2 * n), np.float32)
    first[: h + 1, :n] = c[: h + 1]
    first[part : part + h, :n] = s[:h]
    second = np.concatenate([np.concatenate([c, -s], 1), np.concatenate([-s, -c], 1)], 0)
    inverse = np.concatenate([np.concatenate([c, s], 1), np.concatenate([-s, c], 1)], 0)
    order = (np.arange(n) - h) % n
    last = np.zeros((n, 2 * n), np.float32)
    last[:, 0] = c[order, 0]
    last[:, 1:h] = 2.0 * c[order, 1:h]
    last[:, h] = c[order, h]
    last[:, h + 1 : n] = -2.0 * s[order, 1:h]
    last *= 1.0 / float(n) ** 3
    return np.concatenate([first, second, inverse, last], 0).astype(jnp.bfloat16)


def open_tables(tab, n):
    part = n // 2 + TILE
    first = tab[: 2 * part, :n]
    second = tab[2 * part : 2 * part + 2 * n]
    inverse = tab[2 * part + 2 * n : 2 * part + 4 * n]
    last = tab[2 * part + 4 * n :, :n]
    return (first, second), (inverse, last)


def spectra(x, first, second, put):
    cols, n = x.shape[0], x.shape[-1]
    part = n // 2 + TILE
    lines = []
    for c in range(0, cols, 2):
        y = jnp.dot(
            first, jnp.concatenate([x[c], x[c + 1]], axis=1), preferred_element_type=jnp.float32
        )
        for d in (0, 1):
            mine = y[:, d * n : (d + 1) * n]
            lines.append(jnp.concatenate([mine[:part], mine[part:]], axis=1))
    lines = jnp.concatenate(lines, axis=0).astype(jnp.bfloat16)
    spec = jnp.dot(lines, second, preferred_element_type=jnp.float32)
    for c in range(cols):
        mine = spec[c * part : (c + 1) * part]
        put(c, mine[:, :n], mine[:, n:])


def pairs(get_a, get_b, cols, n, inverse, last, put):
    h = n // 2
    part = h + TILE
    crosses = []
    for c in range(cols):
        a, b = get_a(c), get_b(c)
        ar, ai, br, bi = a[:part], a[part:], b[:part], b[part:]
        real = ar * br + ai * bi
        imag = ar * bi - ai * br
        real_top = real[:TILE] - imag[h:]
        imag_top = imag[:TILE] + real[h:]
        real = jnp.concatenate([real_top, real[TILE:h]], axis=0).astype(jnp.bfloat16)
        imag = jnp.concatenate([imag_top, imag[TILE:h]], axis=0).astype(jnp.bfloat16)
        crosses.append(jnp.concatenate([real, imag], axis=1))
    back = jnp.dot(
        jnp.concatenate(crosses, axis=0), inverse, preferred_element_type=jnp.float32
    ).astype(jnp.bfloat16)
    place = lax.broadcasted_iota(jnp.int32, (TILE, 1), 0).astype(jnp.float32) + float(h)
    for c in range(0, cols, 2):
        sides = []
        for d in (c, c + 1):
            mine = back[d * h : (d + 1) * h]
            sides.append(jnp.concatenate([mine[:, :n], mine[:, n:]], axis=0))
        corr = jnp.dot(last, jnp.concatenate(sides, axis=1), preferred_element_type=jnp.float32)
        power = corr * corr
        total = power[:TILE]
        ramp = total
        for t in range(1, n // TILE):
            total = total + power[t * TILE : (t + 1) * TILE]
            ramp = ramp + total
        shifted = place * total - float(TILE) * ramp
        total = jnp.sum(total, axis=0, keepdims=True)
        shifted = jnp.sum(shifted, axis=0, keepdims=True)
        for d in (0, 1):
            put(c + d, shifted[:, d * n : (d + 1) * n], total[:, d * n : (d + 1) * n])


def left_share(boundary, groups, units):
    return units * (groups - 1 - boundary) // groups


def kernel(
    sizes, patches, tab_in, nodes_in, flags_in, moved, shown,
    tab, x, nodes, flags, from_right, from_left, spec, halo, stats, payload, slots, field, weight,
    tab_sem, small_sem, own_sem, left_send, left_recv, right_send, right_recv, send, recv,
):
    groups, tiles, local, reach, rows, cols, n, width = sizes
    half = LANES // 2
    part = n // 2 + TILE
    span = rows * cols
    parts = cols // width
    heap = rows * parts
    units = reach * heap
    sec = lax.axis_index("sec")
    tile = lax.axis_index("tile")
    me = sec * tiles + tile
    count = groups * tiles
    unroll = count <= 64

    def place(index):
        return (index // tiles, index % tiles)

    barrier = pltpu.get_barrier_semaphore()

    def greet(d, carry):
        pl.semaphore_signal(
            barrier, inc=1, device_id=place((me + d) % count), device_id_type=MESH
        )
        return carry

    lax.fori_loop(1, count, greet, 0, unroll=unroll)

    tab_copy = pltpu.make_async_copy(tab_in, tab, tab_sem)
    tab_copy.start()

    def own_copy(s):
        return pltpu.make_async_copy(patches.at[s], x.at[s], own_sem.at[s])

    for s in range(local):
        own_copy(s).start()
    node_copy = pltpu.make_async_copy(nodes_in, nodes, small_sem.at[0])
    flag_copy = pltpu.make_async_copy(flags_in, flags, small_sem.at[1])
    node_copy.start()
    flag_copy.start()

    has_left = (sec + groups - 1) // groups
    has_right = 1 - (sec + 1) // groups
    sent_left = has_left * left_share(sec - 1, groups, units)
    sent_right = has_right * (units - left_share(sec, groups, units))
    got_right = has_right * left_share(sec, groups, units)
    got_left = has_left * (units - left_share(sec - 1, groups, units))

    def spot(h):
        return h // parts, (h % parts) * width

    def copy_left(k):
        row, col = spot(k % heap)
        return pltpu.make_async_remote_copy(
            src_ref=patches.at[k // heap, row, pl.ds(col, width)],
            dst_ref=from_right.at[k],
            send_sem=left_send.at[k],
            recv_sem=left_recv.at[k],
            device_id=(sec - 1, tile),
            device_id_type=MESH,
        )

    def copy_right(k):
        row, col = spot(heap - 1 - k % heap)
        return pltpu.make_async_remote_copy(
            src_ref=patches.at[local - 1 - k // heap, row, pl.ds(col, width)],
            dst_ref=from_left.at[k],
            send_sem=right_send.at[k],
            recv_sem=right_recv.at[k],
            device_id=(sec + 1, tile),
            device_id_type=MESH,
        )

    stats[...] = jnp.zeros_like(stats)
    payload[...] = jnp.zeros_like(payload)
    pl.semaphore_wait(barrier, count - 1)

    def launch(k, carry):
        @pl.when(k < sent_left)
        def _():
            copy_left(k).start()

        @pl.when(k < sent_right)
        def _():
            copy_right(k).start()

        return carry

    lax.fori_loop(0, units, launch, 0)

    tab_copy.wait()
    forward, inverse = open_tables(tab, n)

    def keep(index, offset, base):
        def put(c, shifted, total):
            at = (offset - 1) * span + base + c
            stats[index, pl.ds(at, 1), :] = shifted
            stats[index, pl.ds(half + at, 1), :] = total

        return put

    def own(s, carry):
        own_copy(s).wait()
        for row in range(rows):

            def put(c, real, imag):
                spec[s, row, c, :part] = real
                spec[s, row, c, part:] = imag

            spectra(x.at[s, row], *forward, put)

        def body(offset, carry):
            for row in range(rows):
                pairs(
                    lambda c: spec[s - offset, row, c],
                    lambda c: spec[s, row, c],
                    cols, n, *inverse, keep(s - offset, offset, row * cols),
                )
            return carry

        return lax.fori_loop(1, jnp.minimum(s, reach) + 1, body, carry)

    lax.fori_loop(0, local, own, 0)

    def put_halo(c, real, imag):
        halo[c, :part] = real
        halo[c, part:] = imag

    def far(k, carry):
        @pl.when(k < got_right)
        def _():
            copy_left(k).wait_recv()
            spectra(from_right.at[k], *forward, put_halo)
            b, h = k // heap, k % heap
            row, col = spot(h)

            def body(a, carry):
                pairs(
                    lambda c: spec[local - 1 - a, row, col + c],
                    lambda c: halo[c],
                    width, n, *inverse, keep(local - 1 - a, a + b + 1, h * width),
                )
                return carry

            lax.fori_loop(0, reach - b, body, 0)

        @pl.when(k < got_left)
        def _():
            copy_right(k).wait_recv()
            spectra(from_left.at[k], *forward, put_halo)
            a, h = k // heap, heap - 1 - k % heap
            row, col = spot(h)
            first = (units - got_left + heap - 1 - h) // heap

            def body(b, carry):
                pairs(
                    lambda c: halo[c],
                    lambda c: spec[b, row, col + c],
                    width, n, *inverse, keep(local + a, a + b + 1, h * width),
                )
                return carry

            lax.fori_loop(first, reach - a, body, 0)

        return carry

    lax.fori_loop(0, jnp.maximum(got_right, got_left), far, 0)

    def sent(k, carry):
        @pl.when(k < sent_left)
        def _():
            copy_left(k).wait_send()

        @pl.when(k < sent_right)
        def _():
            copy_right(k).wait_send()

        return carry

    lax.fori_loop(0, units, sent, 0)

    sub = lax.broadcasted_iota(jnp.int32, (TILE, n), 0)
    lane = lax.broadcasted_iota(jnp.int32, (TILE, n), 1)
    shift = jnp.where(lane < n // 2, lane, lane - n).astype(jnp.float32)
    weigh = jnp.where(sub == 0, 1.0, jnp.where(sub == 1, shift, 0.0))
    node_copy.wait()
    flag_copy.wait()
    area = float(n * n)
    for index in range(local + reach):
        red = lax.dot_general(
            weigh,
            stats[index],
            (((1,), (1,)), ((), ())),
            precision=lax.Precision.HIGHEST,
            preferred_element_type=jnp.float32,
        )
        above, along = red[0:1], red[1:2]
        low = lax.broadcasted_iota(jnp.int32, (1, LANES), 1) < half
        total = jnp.where(low, pltpu.roll(above, half, 1), above) / area + EPSILON
        at = index if index < local else TILE + 2 * local - 1 - index
        payload[at : at + 1] = jnp.where(low, above, along) / area / total
    for comp in range(2):
        for row in range(rows):
            at = comp * half + reach * span + row * cols
            payload[:local, at : at + cols] = nodes[comp, :, row, :]
    for v in range(reach):
        payload[local : local + 1, v * local : (v + 1) * local] = flags[v : v + 1, :].astype(jnp.float32)

    def copy(slot, peer):
        return pltpu.make_async_remote_copy(
            src_ref=payload,
            dst_ref=slots.at[slot],
            send_sem=send.at[peer],
            recv_sem=recv.at[slot],
            device_id=place(peer),
            device_id_type=MESH,
        )

    def start(d, carry):
        copy(me, (me + d) % count).start()
        return carry

    lax.fori_loop(1, count, start, 0, unroll=unroll)
    slots[me] = payload[...]

    def finish(d, carry):
        peer = (me + d) % count
        copy(peer, peer).wait_recv()
        copy(me, peer).wait_send()
        return carry

    lax.fori_loop(1, count, finish, 0, unroll=unroll)

    lane = lax.broadcasted_iota(jnp.int32, (TILE, LANES), 1)
    sub = lax.broadcasted_iota(jnp.int32, (TILE, LANES), 0)
    owner = lane % half // span
    total = groups * local
    for g in range(groups):
        flat = jnp.broadcast_to(slots[g * tiles, local : local + 1], (TILE, LANES))
        for v in range(reach):
            w = jnp.sum(jnp.where(lane == v * local + sub, flat, 0.0), axis=1, keepdims=True)
            w = jnp.broadcast_to(w, (TILE, LANES))
            w = jnp.where(g * local + sub + v + 1 < total, w, 0.0)
            weight[v, g * local : (g + 1) * local, :] = w[:local]
        blocks = []
        for t in range(tiles):
            block = slots[g * tiles + t, :TILE]
            if g < groups - 1:
                block = block + slots[(g + 1) * tiles + t, TILE:]
            blocks.append(block)
        for v in range(reach + 1):
            value = jnp.zeros((TILE, LANES), jnp.float32)
            for t in range(tiles):
                moved_to = blocks[t]
                if t != v:
                    moved_to = pltpu.roll(moved_to, (t - v) * span % LANES, 1)
                value = jnp.where(owner == t, moved_to, value)
            value = value[:local]
            if v < reach:
                value = value * weight[v, g * local : (g + 1) * local, :]
            field[v, g * local : (g + 1) * local, :] = value

    grid_rows = tiles * rows
    at = lax.broadcasted_iota(jnp.int32, (total, LANES), 1) % half
    across = at % cols
    down = at // cols
    one = lambda mask: mask.astype(jnp.float32)
    left, right = one(across > 0), one(across < cols - 1)
    up, below = one(down > 0), one(down < grid_rows - 1)

    def sweep(_, u):
        plane = (
            up * (pltpu.roll(u, cols, 1) - u)
            + below * (pltpu.roll(u, LANES - cols, 1) - u)
            + left * (pltpu.roll(u, 1, 1) - u)
            + right * (pltpu.roll(u, LANES - 1, 1) - u)
        )
        spring = jnp.zeros_like(u)
        for v in range(reach):
            o = v + 1
            r = weight[v] * (pltpu.roll(u, total - o, 0) - u) - field[v]
            spring = spring + r - pltpu.roll(r, o, 0)
        return u + STEP_SIZE * (plane + spring)

    field[reach] = lax.fori_loop(0, SWEEPS, sweep, field[reach])
    back = (LANES - tile * span) % LANES
    for v in range(reach + 1):
        mine = pltpu.roll(field[v, pl.ds(sec * local, local), :], back, 1)
        for comp in range(2):
            for row in range(rows):
                at = comp * half + row * cols
                piece = mine[:, at : at + cols]
                if v < reach:
                    shown[comp, :, v, row, :] = piece
                else:
                    moved[comp, :, row, :] = piece


def shards(patches, pair_flags, nodes):
    local, rows, cols, n = patches.shape[:4]
    reach = pair_flags.shape[1]
    groups, tiles = lax.axis_size("sec"), lax.axis_size("tile")
    part = n // 2 + TILE
    width = cols // 2
    units = reach * rows * cols // width
    tab = jnp.asarray(tables(n))
    sizes = (groups, tiles, local, reach, rows, cols, n, width)
    hbm = pl.BlockSpec(memory_space=pltpu.HBM)
    vmem = pl.BlockSpec(memory_space=pltpu.VMEM)
    dma = pltpu.SemaphoreType.DMA
    return pl.pallas_call(
        functools.partial(kernel, sizes),
        in_specs=[hbm] * 4,
        out_specs=[vmem] * 2,
        out_shape=[
            jax.ShapeDtypeStruct((2, local, rows, cols), jnp.float32),
            jax.ShapeDtypeStruct((2, local, reach, rows, cols), jnp.float32),
        ],
        scratch_shapes=[
            pltpu.VMEM(tab.shape, jnp.bfloat16),
            pltpu.VMEM((local, rows, cols, n, n), jnp.bfloat16),
            pltpu.VMEM(nodes.shape, jnp.float32),
            pltpu.VMEM((reach, local), jnp.int32),
            pltpu.VMEM((units, width, n, n), jnp.bfloat16),
            pltpu.VMEM((units, width, n, n), jnp.bfloat16),
            pltpu.VMEM((local, rows, cols, 2 * part, n), jnp.float32),
            pltpu.VMEM((width, 2 * part, n), jnp.float32),
            pltpu.VMEM((local + reach, LANES, LANES), jnp.float32),
            pltpu.VMEM((2 * TILE, LANES), jnp.float32),
            pltpu.VMEM((groups * tiles, 2 * TILE, LANES), jnp.float32),
            pltpu.VMEM((reach + 1, groups * local, LANES), jnp.float32),
            pltpu.VMEM((reach, groups * local, LANES), jnp.float32),
            dma,
            dma((2,)),
            dma((local,)),
            dma((units,)),
            dma((units,)),
            dma((units,)),
            dma((units,)),
            dma((groups * tiles,)),
            dma((groups * tiles,)),
        ],
        compiler_params=pltpu.CompilerParams(
            collective_id=0, has_side_effects=True, vmem_limit_bytes=65000000
        ),
        name="align",
    )(patches, tab, nodes, pair_flags.T)


def solution(mesh):
    placed = (P("sec", "tile", None, None, None), P("sec", None), P(None, "sec", "tile", None))
    return jax.shard_map(
        shards,
        mesh=mesh,
        in_specs=placed,
        out_specs=(P(None, "sec", "tile", None), P(None, "sec", None, "tile", None)),
        check_vma=False,
    )
```

```python
import functools
import math

import jax
import jax.numpy as jnp
import numpy as np
from jax import lax
from jax.experimental import pallas as pl
from jax.experimental.pallas import tpu as pltpu
from jax.sharding import PartitionSpec as P

SWEEPS = 8
STEP_SIZE = 0.08
EPSILON = 1e-06
LANES = 128
TILE = 8
AHEAD = 4
MESH = pl.DeviceIdType.MESH


def tables(n):
    h = n // 2
    k = np.arange(n)
    phase = (k[:, None] * k[None, :] % n) * (2.0 * math.pi / n)
    c = np.asarray(np.cos(phase), np.float32).astype(jnp.bfloat16).astype(np.float32)
    s = np.asarray(np.sin(phase), np.float32).astype(jnp.bfloat16).astype(np.float32)
    part = h + TILE
    first = np.zeros((2 * part, 2 * n), np.float32)
    first[: h + 1, :n] = c[: h + 1]
    first[part : part + h, :n] = s[:h]
    second = np.concatenate([np.concatenate([c, -s], 1), np.concatenate([-s, -c], 1)], 0)
    inverse = np.concatenate([np.concatenate([c, s], 1), np.concatenate([-s, c], 1)], 0)
    order = (np.arange(n) - h) % n
    last = np.zeros((n, 2 * n), np.float32)
    last[:, 0] = c[order, 0]
    last[:, 1:h] = 2.0 * c[order, 1:h]
    last[:, h] = c[order, h]
    last[:, h + 1 : n] = -2.0 * s[order, 1:h]
    last *= 1.0 / float(n) ** 3
    return np.concatenate([first, second, inverse, last], 0).astype(jnp.bfloat16)


def open_tables(tab, n):
    part = n // 2 + TILE
    first = tab[: 2 * part, :n]
    second = tab[2 * part : 2 * part + 2 * n]
    inverse = tab[2 * part + 2 * n : 2 * part + 4 * n]
    last = tab[2 * part + 4 * n :, :n]
    return (first, second), (inverse, last)


def spectra(x, first, second, put):
    cols, n = x.shape[0], x.shape[-1]
    part = n // 2 + TILE
    lines = []
    for c in range(0, cols, 2):
        y = jnp.dot(
            first, jnp.concatenate([x[c], x[c + 1]], axis=1), preferred_element_type=jnp.float32
        )
        for d in (0, 1):
            mine = y[:, d * n : (d + 1) * n]
            lines.append(jnp.concatenate([mine[:part], mine[part:]], axis=1))
    lines = jnp.concatenate(lines, axis=0).astype(jnp.bfloat16)
    spec = jnp.dot(lines, second, preferred_element_type=jnp.float32)
    for c in range(cols):
        mine = spec[c * part : (c + 1) * part]
        put(c, mine[:, :n], mine[:, n:])


def pairs(get_a, get_b, cols, n, inverse, last, put):
    h = n // 2
    part = h + TILE
    crosses = []
    for c in range(cols):
        a, b = get_a(c), get_b(c)
        ar, ai, br, bi = a[:part], a[part:], b[:part], b[part:]
        real = ar * br + ai * bi
        imag = ar * bi - ai * br
        real_top = real[:TILE] - imag[h:]
        imag_top = imag[:TILE] + real[h:]
        real = jnp.concatenate([real_top, real[TILE:h]], axis=0).astype(jnp.bfloat16)
        imag = jnp.concatenate([imag_top, imag[TILE:h]], axis=0).astype(jnp.bfloat16)
        crosses.append(jnp.concatenate([real, imag], axis=1))
    back = jnp.dot(
        jnp.concatenate(crosses, axis=0), inverse, preferred_element_type=jnp.float32
    ).astype(jnp.bfloat16)
    place = lax.broadcasted_iota(jnp.int32, (TILE, 1), 0).astype(jnp.float32) + float(h)
    for c in range(0, cols, 2):
        sides = []
        for d in (c, c + 1):
            mine = back[d * h : (d + 1) * h]
            sides.append(jnp.concatenate([mine[:, :n], mine[:, n:]], axis=0))
        corr = jnp.dot(last, jnp.concatenate(sides, axis=1), preferred_element_type=jnp.float32)
        power = corr * corr
        total = power[:TILE]
        ramp = total
        for t in range(1, n // TILE):
            total = total + power[t * TILE : (t + 1) * TILE]
            ramp = ramp + total
        shifted = place * total - float(TILE) * ramp
        total = jnp.sum(total, axis=0, keepdims=True)
        shifted = jnp.sum(shifted, axis=0, keepdims=True)
        for d in (0, 1):
            put(c + d, shifted[:, d * n : (d + 1) * n], total[:, d * n : (d + 1) * n])


def left_share(boundary, groups, units):
    return units * (groups - 1 - boundary) // groups


def kernel(
    sizes, patches, tab_in, nodes_in, flags_in, moved, shown,
    tab, x, nodes, flags, from_right, from_left, spec, halo, stats, payload, slots, field, weight,
    tab_sem, small_sem, own_sem, left_send, left_recv, right_send, right_recv, send, recv, chain,
):
    groups, tiles, local, reach, rows, cols, n, width = sizes
    half = LANES // 2
    part = n // 2 + TILE
    span = rows * cols
    parts = cols // width
    heap = rows * parts
    units = reach * heap
    sec = lax.axis_index("sec")
    tile = lax.axis_index("tile")
    me = sec * tiles + tile
    count = groups * tiles
    unroll = count <= 64

    def place(index):
        return (index // tiles, index % tiles)

    barrier = pltpu.get_barrier_semaphore()

    for d in range(1, tiles):
        pl.semaphore_signal(
            barrier, inc=1, device_id=(sec, (tile + d) % tiles), device_id_type=MESH
        )

    @pl.when(sec > 0)
    def _():
        pl.semaphore_signal(barrier, inc=1, device_id=(sec - 1, tile), device_id_type=MESH)

    @pl.when(sec < groups - 1)
    def _():
        pl.semaphore_signal(barrier, inc=1, device_id=(sec + 1, tile), device_id_type=MESH)

    tab_copy = pltpu.make_async_copy(tab_in, tab, tab_sem)
    tab_copy.start()

    def own_copy(s):
        return pltpu.make_async_copy(patches.at[s], x.at[s], own_sem.at[s])

    for s in range(local):
        own_copy(s).start()
    node_copy = pltpu.make_async_copy(nodes_in, nodes, small_sem.at[0])
    flag_copy = pltpu.make_async_copy(flags_in, flags, small_sem.at[1])
    node_copy.start()
    flag_copy.start()

    has_left = (sec + groups - 1) // groups
    has_right = 1 - (sec + 1) // groups
    sent_left = has_left * left_share(sec - 1, groups, units)
    sent_right = has_right * (units - left_share(sec, groups, units))
    got_right = has_right * left_share(sec, groups, units)
    got_left = has_left * (units - left_share(sec - 1, groups, units))

    def spot(h):
        return h // parts, (h % parts) * width

    def copy_left(k):
        row, col = spot(k % heap)
        return pltpu.make_async_remote_copy(
            src_ref=patches.at[k // heap, row, pl.ds(col, width)],
            dst_ref=from_right.at[k],
            send_sem=left_send.at[k],
            recv_sem=left_recv.at[k],
            device_id=(sec - 1, tile),
            device_id_type=MESH,
        )

    def copy_right(k):
        row, col = spot(heap - 1 - k % heap)
        return pltpu.make_async_remote_copy(
            src_ref=patches.at[local - 1 - k // heap, row, pl.ds(col, width)],
            dst_ref=from_left.at[k],
            send_sem=right_send.at[k],
            recv_sem=right_recv.at[k],
            device_id=(sec + 1, tile),
            device_id_type=MESH,
        )

    stats[...] = jnp.zeros_like(stats)
    payload[...] = jnp.zeros_like(payload)
    pl.semaphore_wait(barrier, tiles - 1 + has_left + has_right)

    late = left_share(sec, groups, units) - 1

    def launch(k, carry):
        @pl.when(k < sent_left)
        def _():
            copy_left(k).start()

        @pl.when((k >= late) & (k - late < sent_right))
        def _():
            copy_right(k - late).start()

        return carry

    def tell():
        @pl.when(sec > 0)
        def _():
            pl.semaphore_signal(chain.at[1], inc=1, device_id=(sec - 1, tile), device_id_type=MESH)

        @pl.when(sec < groups - 1)
        def _():
            pl.semaphore_signal(chain.at[0], inc=1, device_id=(sec + 1, tile), device_id_type=MESH)

    rounds = groups - 2

    def relay(s, carry):
        @pl.when((s < rounds) & (sec > 0))
        def _():
            pl.semaphore_wait(chain.at[0], 1)

        @pl.when((s < rounds) & (sec < groups - 1))
        def _():
            pl.semaphore_wait(chain.at[1], 1)

        @pl.when(s + 1 < rounds)
        def _():
            tell()

        return carry

    launch(0, 0)
    if rounds > 0:
        tell()

    tab_copy.wait()
    forward, inverse = open_tables(tab, n)

    def keep(index, offset, base):
        def put(c, shifted, total):
            at = (offset - 1) * span + base + c
            stats[index, pl.ds(at, 1), :] = shifted
            stats[index, pl.ds(half + at, 1), :] = total

        return put

    def own(s, carry):
        @pl.when(s > 0)
        def _():
            launch(s, 0)

        own_copy(s).wait()
        for row in range(rows):

            def put(c, real, imag):
                spec[s, row, c, :part] = real
                spec[s, row, c, part:] = imag

            spectra(x.at[s, row], *forward, put)

        def body(offset, carry):
            for row in range(rows):
                pairs(
                    lambda c: spec[s - offset, row, c],
                    lambda c: spec[s, row, c],
                    cols, n, *inverse, keep(s - offset, offset, row * cols),
                )
            return carry

        lax.fori_loop(1, jnp.minimum(s, reach) + 1, body, 0)
        return relay(s, carry)

    lax.fori_loop(0, local, own, 0)
    lax.fori_loop(local, rounds, relay, 0)

    def put_halo(c, real, imag):
        halo[c, :part] = real
        halo[c, part:] = imag

    def far(k, carry):
        @pl.when(k + AHEAD >= local)
        def _():
            launch(k + AHEAD, 0)

        @pl.when(k < got_right)
        def _():
            copy_left(k).wait_recv()
            spectra(from_right.at[k], *forward, put_halo)
            b, h = k // heap, k % heap
            row, col = spot(h)

            def body(a, carry):
                pairs(
                    lambda c: spec[local - 1 - a, row, col + c],
                    lambda c: halo[c],
                    width, n, *inverse, keep(local - 1 - a, a + b + 1, h * width),
                )
                return carry

            lax.fori_loop(0, reach - b, body, 0)

        @pl.when(k >= got_right)
        def _():
            u = k - got_right
            copy_right(u).wait_recv()
            spectra(from_left.at[u], *forward, put_halo)
            a, h = u // heap, heap - 1 - u % heap
            row, col = spot(h)
            first = (units - got_left + heap - 1 - h) // heap

            def body(b, carry):
                pairs(
                    lambda c: halo[c],
                    lambda c: spec[b, row, col + c],
                    width, n, *inverse, keep(local + a, a + b + 1, h * width),
                )
                return carry

            lax.fori_loop(first, reach - a, body, 0)

        return carry

    got = got_right + got_left
    lax.fori_loop(0, got, far, 0)
    lax.fori_loop(jnp.maximum(local, got + AHEAD), 2 * units, launch, 0)

    def sent(k, carry):
        @pl.when(k < sent_left)
        def _():
            copy_left(k).wait_send()

        @pl.when(k < sent_right)
        def _():
            copy_right(k).wait_send()

        return carry

    lax.fori_loop(0, units, sent, 0)

    sub = lax.broadcasted_iota(jnp.int32, (TILE, n), 0)
    lane = lax.broadcasted_iota(jnp.int32, (TILE, n), 1)
    shift = jnp.where(lane < n // 2, lane, lane - n).astype(jnp.float32)
    weigh = jnp.where(sub == 0, 1.0, jnp.where(sub == 1, shift, 0.0))
    node_copy.wait()
    flag_copy.wait()
    area = float(n * n)
    for index in range(local + reach):
        red = lax.dot_general(
            weigh,
            stats[index],
            (((1,), (1,)), ((), ())),
            precision=lax.Precision.HIGHEST,
            preferred_element_type=jnp.float32,
        )
        above, along = red[0:1], red[1:2]
        low = lax.broadcasted_iota(jnp.int32, (1, LANES), 1) < half
        total = jnp.where(low, pltpu.roll(above, half, 1), above) / area + EPSILON
        at = index if index < local else TILE + 2 * local - 1 - index
        payload[at : at + 1] = jnp.where(low, above, along) / area / total
    for comp in range(2):
        for row in range(rows):
            at = comp * half + reach * span + row * cols
            payload[:local, at : at + cols] = nodes[comp, :, row, :]
    for v in range(reach):
        payload[local : local + 1, v * local : (v + 1) * local] = flags[v : v + 1, :].astype(jnp.float32)

    def copy(slot, peer):
        return pltpu.make_async_remote_copy(
            src_ref=payload,
            dst_ref=slots.at[slot],
            send_sem=send.at[peer],
            recv_sem=recv.at[slot],
            device_id=place(peer),
            device_id_type=MESH,
        )

    def start(d, carry):
        copy(me, (me + d) % count).start()
        return carry

    lax.fori_loop(1, count, start, 0, unroll=unroll)
    slots[me] = payload[...]

    def finish(d, carry):
        peer = (me + d) % count
        copy(peer, peer).wait_recv()
        copy(me, peer).wait_send()
        return carry

    lax.fori_loop(1, count, finish, 0, unroll=unroll)

    lane = lax.broadcasted_iota(jnp.int32, (TILE, LANES), 1)
    sub = lax.broadcasted_iota(jnp.int32, (TILE, LANES), 0)
    owner = lane % half // span
    total = groups * local
    for g in range(groups):
        flat = jnp.broadcast_to(slots[g * tiles, local : local + 1], (TILE, LANES))
        for v in range(reach):
            w = jnp.sum(jnp.where(lane == v * local + sub, flat, 0.0), axis=1, keepdims=True)
            w = jnp.broadcast_to(w, (TILE, LANES))
            w = jnp.where(g * local + sub + v + 1 < total, w, 0.0)
            weight[v, g * local : (g + 1) * local, :] = w[:local]
        blocks = []
        for t in range(tiles):
            block = slots[g * tiles + t, :TILE]
            if g < groups - 1:
                block = block + slots[(g + 1) * tiles + t, TILE:]
            blocks.append(block)
        for v in range(reach + 1):
            value = jnp.zeros((TILE, LANES), jnp.float32)
            for t in range(tiles):
                moved_to = blocks[t]
                if t != v:
                    moved_to = pltpu.roll(moved_to, (t - v) * span % LANES, 1)
                value = jnp.where(owner == t, moved_to, value)
            value = value[:local]
            if v < reach:
                value = value * weight[v, g * local : (g + 1) * local, :]
            field[v, g * local : (g + 1) * local, :] = value

    grid_rows = tiles * rows
    at = lax.broadcasted_iota(jnp.int32, (total, LANES), 1) % half
    across = at % cols
    down = at // cols
    one = lambda mask: mask.astype(jnp.float32)
    left, right = one(across > 0), one(across < cols - 1)
    up, below = one(down > 0), one(down < grid_rows - 1)

    def sweep(_, u):
        plane = (
            up * (pltpu.roll(u, cols, 1) - u)
            + below * (pltpu.roll(u, LANES - cols, 1) - u)
            + left * (pltpu.roll(u, 1, 1) - u)
            + right * (pltpu.roll(u, LANES - 1, 1) - u)
        )
        spring = jnp.zeros_like(u)
        for v in range(reach):
            o = v + 1
            r = weight[v] * (pltpu.roll(u, total - o, 0) - u) - field[v]
            spring = spring + r - pltpu.roll(r, o, 0)
        return u + STEP_SIZE * (plane + spring)

    field[reach] = lax.fori_loop(0, SWEEPS, sweep, field[reach])
    back = (LANES - tile * span) % LANES
    for v in range(reach + 1):
        mine = pltpu.roll(field[v, pl.ds(sec * local, local), :], back, 1)
        for comp in range(2):
            for row in range(rows):
                at = comp * half + row * cols
                piece = mine[:, at : at + cols]
                if v < reach:
                    shown[comp, :, v, row, :] = piece
                else:
                    moved[comp, :, row, :] = piece


def shards(patches, pair_flags, nodes):
    local, rows, cols, n = patches.shape[:4]
    reach = pair_flags.shape[1]
    groups, tiles = lax.axis_size("sec"), lax.axis_size("tile")
    part = n // 2 + TILE
    width = cols // 2
    units = reach * rows * cols // width
    tab = jnp.asarray(tables(n))
    sizes = (groups, tiles, local, reach, rows, cols, n, width)
    hbm = pl.BlockSpec(memory_space=pltpu.HBM)
    vmem = pl.BlockSpec(memory_space=pltpu.VMEM)
    dma = pltpu.SemaphoreType.DMA
    return pl.pallas_call(
        functools.partial(kernel, sizes),
        in_specs=[hbm] * 4,
        out_specs=[vmem] * 2,
        out_shape=[
            jax.ShapeDtypeStruct((2, local, rows, cols), jnp.float32),
            jax.ShapeDtypeStruct((2, local, reach, rows, cols), jnp.float32),
        ],
        scratch_shapes=[
            pltpu.VMEM(tab.shape, jnp.bfloat16),
            pltpu.VMEM((local, rows, cols, n, n), jnp.bfloat16),
            pltpu.VMEM(nodes.shape, jnp.float32),
            pltpu.VMEM((reach, local), jnp.int32),
            pltpu.VMEM((units, width, n, n), jnp.bfloat16),
            pltpu.VMEM((units, width, n, n), jnp.bfloat16),
            pltpu.VMEM((local, rows, cols, 2 * part, n), jnp.float32),
            pltpu.VMEM((width, 2 * part, n), jnp.float32),
            pltpu.VMEM((local + reach, LANES, LANES), jnp.float32),
            pltpu.VMEM((2 * TILE, LANES), jnp.float32),
            pltpu.VMEM((groups * tiles, 2 * TILE, LANES), jnp.float32),
            pltpu.VMEM((reach + 1, groups * local, LANES), jnp.float32),
            pltpu.VMEM((reach, groups * local, LANES), jnp.float32),
            dma,
            dma((2,)),
            dma((local,)),
            dma((units,)),
            dma((units,)),
            dma((units,)),
            dma((units,)),
            dma((groups * tiles,)),
            dma((groups * tiles,)),
            pltpu.SemaphoreType.REGULAR((2,)),
        ],
        compiler_params=pltpu.CompilerParams(
            collective_id=0, has_side_effects=True, vmem_limit_bytes=(64 << 20) - (160 << 10)
        ),
        name="align",
    )(patches, tab, nodes, pair_flags.T)


def solution(mesh):
    placed = (P("sec", "tile", None, None, None), P("sec", None), P(None, "sec", "tile", None))
    return jax.shard_map(
        shards,
        mesh=mesh,
        in_specs=placed,
        out_specs=(P(None, "sec", "tile", None), P(None, "sec", None, "tile", None)),
        check_vma=False,
    )
```

```python
import functools
import math

import jax
import jax.numpy as jnp
import numpy as np
from jax import lax
from jax.experimental import pallas as pl
from jax.experimental.pallas import tpu as pltpu
from jax.sharding import PartitionSpec as P

SWEEPS = 8
STEP_SIZE = 0.08
EPSILON = 1e-06
LANES = 128
TILE = 8
MESH = pl.DeviceIdType.MESH


def tables(n):
    h = n // 2
    k = np.arange(n)
    phase = (k[:, None] * k[None, :] % n) * (2.0 * math.pi / n)
    c = np.asarray(np.cos(phase), np.float32).astype(jnp.bfloat16).astype(np.float32)
    s = np.asarray(np.sin(phase), np.float32).astype(jnp.bfloat16).astype(np.float32)
    part = h + TILE
    first = np.zeros((2 * part, 2 * n), np.float32)
    first[: h + 1, :n] = c[: h + 1]
    first[part : part + h, :n] = s[:h]
    second = np.concatenate([np.concatenate([c, -s], 1), np.concatenate([-s, -c], 1)], 0)
    inverse = np.concatenate([np.concatenate([c, s], 1), np.concatenate([-s, c], 1)], 0)
    order = (np.arange(n) - h) % n
    last = np.zeros((n, 2 * n), np.float32)
    last[:, 0] = c[order, 0]
    last[:, 1:h] = 2.0 * c[order, 1:h]
    last[:, h] = c[order, h]
    last[:, h + 1 : n] = -2.0 * s[order, 1:h]
    last *= 1.0 / float(n) ** 3
    return np.concatenate([first, second, inverse, last], 0).astype(jnp.bfloat16)


def open_tables(tab, n):
    part = n // 2 + TILE
    first = tab[: 2 * part, :n]
    second = tab[2 * part : 2 * part + 2 * n]
    inverse = tab[2 * part + 2 * n : 2 * part + 4 * n]
    last = tab[2 * part + 4 * n :, :n]
    return (first, second), (inverse, last)


def spectra(x, first, second, put):
    cols, n = x.shape[0], x.shape[-1]
    part = n // 2 + TILE
    lines = []
    for c in range(0, cols, 2):
        y = jnp.dot(
            first, jnp.concatenate([x[c], x[c + 1]], axis=1), preferred_element_type=jnp.float32
        )
        for d in (0, 1):
            mine = y[:, d * n : (d + 1) * n]
            lines.append(jnp.concatenate([mine[:part], mine[part:]], axis=1))
    lines = jnp.concatenate(lines, axis=0).astype(jnp.bfloat16)
    spec = jnp.dot(lines, second, preferred_element_type=jnp.float32)
    for c in range(cols):
        mine = spec[c * part : (c + 1) * part]
        put(c, mine[:, :n], mine[:, n:])


def pairs(get_a, get_b, cols, n, inverse, last, put):
    h = n // 2
    part = h + TILE
    crosses = []
    for c in range(cols):
        a, b = get_a(c), get_b(c)
        ar, ai, br, bi = a[:part], a[part:], b[:part], b[part:]
        real = ar * br + ai * bi
        imag = ar * bi - ai * br
        real_top = real[:TILE] - imag[h:]
        imag_top = imag[:TILE] + real[h:]
        real = jnp.concatenate([real_top, real[TILE:h]], axis=0).astype(jnp.bfloat16)
        imag = jnp.concatenate([imag_top, imag[TILE:h]], axis=0).astype(jnp.bfloat16)
        crosses.append(jnp.concatenate([real, imag], axis=1))
    back = jnp.dot(
        jnp.concatenate(crosses, axis=0), inverse, preferred_element_type=jnp.float32
    ).astype(jnp.bfloat16)
    place = lax.broadcasted_iota(jnp.int32, (TILE, 1), 0).astype(jnp.float32) + float(h)
    for c in range(0, cols, 2):
        sides = []
        for d in (c, c + 1):
            mine = back[d * h : (d + 1) * h]
            sides.append(jnp.concatenate([mine[:, :n], mine[:, n:]], axis=0))
        corr = jnp.dot(last, jnp.concatenate(sides, axis=1), preferred_element_type=jnp.float32)
        power = corr * corr
        total = power[:TILE]
        ramp = total
        for t in range(1, n // TILE):
            total = total + power[t * TILE : (t + 1) * TILE]
            ramp = ramp + total
        shifted = place * total - float(TILE) * ramp
        total = jnp.sum(total, axis=0, keepdims=True)
        shifted = jnp.sum(shifted, axis=0, keepdims=True)
        for d in (0, 1):
            put(c + d, shifted[:, d * n : (d + 1) * n], total[:, d * n : (d + 1) * n])


def left_share(boundary, groups, units):
    return units * (groups - 1 - boundary) // groups


def kernel(
    sizes, patches, tab_in, nodes_in, flags_in, moved, shown,
    tab, x, nodes, flags, from_right, from_left, spec, halo, stats, payload, slots, field, weight,
    tab_sem, small_sem, own_sem, left_send, left_recv, right_send, right_recv, send, recv, chain,
):
    groups, tiles, local, reach, rows, cols, n, width = sizes
    half = LANES // 2
    part = n // 2 + TILE
    span = rows * cols
    parts = cols // width
    heap = rows * parts
    units = reach * heap
    sec = lax.axis_index("sec")
    tile = lax.axis_index("tile")
    me = sec * tiles + tile
    count = groups * tiles

    def place(index):
        return (index // tiles, index % tiles)

    slots[...] = jnp.zeros_like(slots)
    barrier = pltpu.get_barrier_semaphore()

    for d in range(1, tiles):
        pl.semaphore_signal(
            barrier, inc=1, device_id=(sec, (tile + d) % tiles), device_id_type=MESH
        )

    @pl.when(sec > 0)
    def _():
        pl.semaphore_signal(barrier, inc=1, device_id=(sec - 1, tile), device_id_type=MESH)

    @pl.when(sec < groups - 1)
    def _():
        pl.semaphore_signal(barrier, inc=1, device_id=(sec + 1, tile), device_id_type=MESH)

    tab_copy = pltpu.make_async_copy(tab_in, tab, tab_sem)
    tab_copy.start()

    def own_copy(s):
        return pltpu.make_async_copy(patches.at[s], x.at[s], own_sem.at[s])

    for s in range(local):
        own_copy(s).start()
    node_copy = pltpu.make_async_copy(nodes_in, nodes, small_sem.at[0])
    flag_copy = pltpu.make_async_copy(flags_in, flags, small_sem.at[1])
    node_copy.start()
    flag_copy.start()

    halves = 2 * units
    has_left = (sec + groups - 1) // groups
    has_right = 1 - (sec + 1) // groups
    near = left_share(sec, groups, halves)
    before = left_share(sec - 1, groups, halves)
    sent_left = has_left * ((before + 1) // 2)
    sent_right = has_right * ((halves - near + 1) // 2)
    got_right = has_right * ((near + 1) // 2)
    got_left = has_left * ((halves - before + 1) // 2)
    odd_near, odd_before = near % 2, before % 2

    def spot(h):
        return h // parts, (h % parts) * width

    def copy_left(k, size):
        row, col = spot(k % heap)
        return pltpu.make_async_remote_copy(
            src_ref=patches.at[k // heap, row, pl.ds(col, size)],
            dst_ref=from_right.at[k, pl.ds(0, size)],
            send_sem=left_send.at[k],
            recv_sem=left_recv.at[k],
            device_id=(sec - 1, tile),
            device_id_type=MESH,
        )

    def copy_right(k, size):
        row, col = spot(heap - 1 - k % heap)
        rest = width - size
        return pltpu.make_async_remote_copy(
            src_ref=patches.at[local - 1 - k // heap, row, pl.ds(col + rest, size)],
            dst_ref=from_left.at[k, pl.ds(rest, size)],
            send_sem=right_send.at[k],
            recv_sem=right_recv.at[k],
            device_id=(sec + 1, tile),
            device_id_type=MESH,
        )

    def each(copy, act, k, count, odd):
        part_unit = (odd == 1) & (k == count - 1)

        @pl.when((k >= 0) & (k < count) & jnp.logical_not(part_unit))
        def _():
            act(copy(k, width))

        @pl.when(part_unit)
        def _():
            act(copy(k, width // 2))

    stats[...] = jnp.zeros_like(stats)
    pl.semaphore_wait(barrier, tiles - 1 + has_left + has_right)

    begin = lambda copy: copy.start()

    def launch(k, carry):
        each(copy_left, begin, k, sent_left, odd_before)
        each(copy_right, begin, k, sent_right, odd_near)
        return carry

    def tell():
        @pl.when(sec > 0)
        def _():
            pl.semaphore_signal(chain.at[1], inc=1, device_id=(sec - 1, tile), device_id_type=MESH)

        @pl.when(sec < groups - 1)
        def _():
            pl.semaphore_signal(chain.at[0], inc=1, device_id=(sec + 1, tile), device_id_type=MESH)

    rounds = groups - 2

    def relay(s, carry):
        @pl.when((s < rounds) & (sec > 0))
        def _():
            pl.semaphore_wait(chain.at[0], 1)

        @pl.when((s < rounds) & (sec < groups - 1))
        def _():
            pl.semaphore_wait(chain.at[1], 1)

        @pl.when(s + 1 < rounds)
        def _():
            tell()

        return carry

    lax.fori_loop(0, units, launch, 0)
    if rounds > 0:
        tell()

    tab_copy.wait()
    forward, inverse = open_tables(tab, n)

    def keep(index, offset, base, low=None, high=None):
        def put(c, shifted, total):
            valid = low if c < width // 2 else high
            if valid is not None:
                shifted = jnp.where(valid, shifted, 0.0)
                total = jnp.where(valid, total, 0.0)
            at = (offset - 1) * span + base + c
            stats[index, pl.ds(at, 1), :] = shifted
            stats[index, pl.ds(half + at, 1), :] = total

        return put

    def own(s, carry):
        own_copy(s).wait()
        for row in range(rows):

            def put(c, real, imag):
                spec[s, row, c, :part] = real
                spec[s, row, c, part:] = imag

            spectra(x.at[s, row], *forward, put)

        def body(offset, carry):
            for row in range(rows):
                pairs(
                    lambda c: spec[s - offset, row, c],
                    lambda c: spec[s, row, c],
                    cols, n, *inverse, keep(s - offset, offset, row * cols),
                )
            return carry

        lax.fori_loop(1, jnp.minimum(s, reach) + 1, body, 0)
        return relay(s, carry)

    lax.fori_loop(0, local, own, 0)
    lax.fori_loop(local, rounds, relay, 0)

    def put_halo(c, real, imag):
        halo[c, :part] = real
        halo[c, part:] = imag

    def far(k, carry):
        odd = sec % 2
        u = k - odd * got_right
        k = k - (1 - odd) * got_left

        @pl.when((k >= 0) & (k < got_right))
        def _():
            each(copy_left, lambda copy: copy.wait_recv(), k, got_right, odd_near)
            spectra(from_right.at[k], *forward, put_halo)
            b, h = k // heap, k % heap
            row, col = spot(h)
            whole = (odd_near == 0) | (k < got_right - 1)

            def body(a, carry):
                pairs(
                    lambda c: spec[local - 1 - a, row, col + c],
                    lambda c: halo[c],
                    width, n, *inverse, keep(local - 1 - a, a + b + 1, h * width, None, whole),
                )
                return carry

            lax.fori_loop(0, reach - b, body, 0)

        @pl.when((u >= 0) & (u < got_left))
        def _():
            each(copy_right, lambda copy: copy.wait_recv(), u, got_left, odd_before)
            spectra(from_left.at[u], *forward, put_halo)
            a, h = u // heap, heap - 1 - u % heap
            row, col = spot(h)
            first = (before // 2 + heap - 1 - h) // heap

            def body(b, carry):
                whole = (odd_before == 0) | (b * heap + h > before // 2)
                pairs(
                    lambda c: halo[c],
                    lambda c: spec[b, row, col + c],
                    width, n, *inverse, keep(local + a, a + b + 1, h * width, whole, None),
                )
                return carry

            lax.fori_loop(first, reach - a, body, 0)

        return carry

    got = got_right + got_left
    lax.fori_loop(0, got, far, 0)

    def sent(k, carry):
        done = lambda copy: copy.wait_send()
        each(copy_left, done, k, sent_left, odd_before)
        each(copy_right, done, k, sent_right, odd_near)
        return carry

    lax.fori_loop(0, units, sent, 0)

    sub = lax.broadcasted_iota(jnp.int32, (TILE, n), 0)
    lane = lax.broadcasted_iota(jnp.int32, (TILE, n), 1)
    shift = jnp.where(lane < n // 2, lane, lane - n).astype(jnp.float32)
    weigh = jnp.where(sub == 0, 1.0, jnp.where(sub == 1, shift, 0.0))
    node_copy.wait()
    flag_copy.wait()
    area = float(n * n)
    for index in range(local + reach):
        red = lax.dot_general(
            weigh,
            stats[index],
            (((1,), (1,)), ((), ())),
            precision=lax.Precision.HIGHEST,
            preferred_element_type=jnp.float32,
        )
        above, along = red[0:1], red[1:2]
        low = lax.broadcasted_iota(jnp.int32, (1, LANES), 1) < half
        total = jnp.where(low, pltpu.roll(above, half, 1), above) / area + EPSILON
        at = index if index < local else 2 * local + reach - index
        payload[at : at + 1] = jnp.where(low, above, along) / area / total
    for comp in range(2):
        for row in range(rows):
            at = comp * half + reach * span + row * cols
            payload[:local, at : at + cols] = nodes[comp, :, row, :]
    for v in range(reach):
        payload[local : local + 1, v * local : (v + 1) * local] = flags[v : v + 1, :].astype(jnp.float32)

    def copy(slot, peer):
        return pltpu.make_async_remote_copy(
            src_ref=payload,
            dst_ref=slots.at[slot],
            send_sem=send.at[peer],
            recv_sem=recv.at[slot],
            device_id=place(peer),
            device_id_type=MESH,
        )

    span_of = 2 * min(groups - 1, -(-SWEEPS * reach // local)) + 1
    others = span_of * tiles

    def peers(act):
        def visit(d, carry):
            to = sec + d // tiles - span_of // 2
            peer = to * tiles + d % tiles

            @pl.when((to >= 0) & (to < groups) & (peer != me))
            def _():
                act(peer)

            return carry

        lax.fori_loop(0, others, visit, 0, unroll=others <= 64)

    peers(lambda peer: copy(me, peer).start())
    slots[me] = payload[...]

    def finish(peer):
        copy(peer, peer).wait_recv()
        copy(me, peer).wait_send()

    peers(finish)

    lane = lax.broadcasted_iota(jnp.int32, (TILE, LANES), 1)
    sub = lax.broadcasted_iota(jnp.int32, (TILE, LANES), 0)
    owner = lane % half // span
    total = groups * local
    for g in range(groups):
        flat = jnp.broadcast_to(slots[g * tiles, local : local + 1], (TILE, LANES))
        for v in range(reach):
            w = jnp.sum(jnp.where(lane == v * local + sub, flat, 0.0), axis=1, keepdims=True)
            w = jnp.broadcast_to(w, (TILE, LANES))
            w = jnp.where(g * local + sub + v + 1 < total, w, 0.0)
            weight[v, g * local : (g + 1) * local, :] = w[:local]
        blocks = []
        for t in range(tiles):
            block = slots[g * tiles + t, :local]
            if g < groups - 1:
                add = slots[(g + 1) * tiles + t, local + 1 :]
                block = jnp.concatenate([block[: local - reach], block[local - reach :] + add], axis=0)
            blocks.append(jnp.concatenate([block, jnp.zeros((TILE - local, LANES), jnp.float32)], axis=0))
        for v in range(reach + 1):
            value = jnp.zeros((TILE, LANES), jnp.float32)
            for t in range(tiles):
                moved_to = blocks[t]
                if t != v:
                    moved_to = pltpu.roll(moved_to, (t - v) * span % LANES, 1)
                value = jnp.where(owner == t, moved_to, value)
            value = value[:local]
            if v < reach:
                value = value * weight[v, g * local : (g + 1) * local, :]
            field[v, g * local : (g + 1) * local, :] = value

    grid_rows = tiles * rows
    at = lax.broadcasted_iota(jnp.int32, (total, LANES), 1) % half
    across = at % cols
    down = at // cols
    one = lambda mask: mask.astype(jnp.float32)
    left, right = one(across > 0), one(across < cols - 1)
    up, below = one(down > 0), one(down < grid_rows - 1)

    def sweep(_, u):
        plane = (
            up * (pltpu.roll(u, cols, 1) - u)
            + below * (pltpu.roll(u, LANES - cols, 1) - u)
            + left * (pltpu.roll(u, 1, 1) - u)
            + right * (pltpu.roll(u, LANES - 1, 1) - u)
        )
        spring = jnp.zeros_like(u)
        for v in range(reach):
            o = v + 1
            r = weight[v] * (pltpu.roll(u, total - o, 0) - u) - field[v]
            spring = spring + r - pltpu.roll(r, o, 0)
        return u + STEP_SIZE * (plane + spring)

    field[reach] = lax.fori_loop(0, SWEEPS, sweep, field[reach])
    back = (LANES - tile * span) % LANES
    for v in range(reach + 1):
        mine = pltpu.roll(field[v, pl.ds(sec * local, local), :], back, 1)
        for comp in range(2):
            for row in range(rows):
                at = comp * half + row * cols
                piece = mine[:, at : at + cols]
                if v < reach:
                    shown[comp, :, v, row, :] = piece
                else:
                    moved[comp, :, row, :] = piece


def shards(patches, pair_flags, nodes):
    local, rows, cols, n = patches.shape[:4]
    reach = pair_flags.shape[1]
    groups, tiles = lax.axis_size("sec"), lax.axis_size("tile")
    part = n // 2 + TILE
    width = cols // 2
    units = reach * rows * cols // width
    tab = jnp.asarray(tables(n))
    sizes = (groups, tiles, local, reach, rows, cols, n, width)
    hbm = pl.BlockSpec(memory_space=pltpu.HBM)
    vmem = pl.BlockSpec(memory_space=pltpu.VMEM)
    dma = pltpu.SemaphoreType.DMA
    return pl.pallas_call(
        functools.partial(kernel, sizes),
        in_specs=[hbm] * 4,
        out_specs=[vmem] * 2,
        out_shape=[
            jax.ShapeDtypeStruct((2, local, rows, cols), jnp.float32),
            jax.ShapeDtypeStruct((2, local, reach, rows, cols), jnp.float32),
        ],
        scratch_shapes=[
            pltpu.VMEM(tab.shape, jnp.bfloat16),
            pltpu.VMEM((local, rows, cols, n, n), jnp.bfloat16),
            pltpu.VMEM(nodes.shape, jnp.float32),
            pltpu.VMEM((reach, local), jnp.int32),
            pltpu.VMEM((units, width, n, n), jnp.bfloat16),
            pltpu.VMEM((units, width, n, n), jnp.bfloat16),
            pltpu.VMEM((local, rows, cols, 2 * part, n), jnp.float32),
            pltpu.VMEM((width, 2 * part, n), jnp.float32),
            pltpu.VMEM((local + reach, LANES, LANES), jnp.float32),
            pltpu.VMEM((local + reach + 1, LANES), jnp.float32),
            pltpu.VMEM((groups * tiles, local + reach + 1, LANES), jnp.float32),
            pltpu.VMEM((reach + 1, groups * local, LANES), jnp.float32),
            pltpu.VMEM((reach, groups * local, LANES), jnp.float32),
            dma,
            dma((2,)),
            dma((local,)),
            dma((units,)),
            dma((units,)),
            dma((units,)),
            dma((units,)),
            dma((groups * tiles,)),
            dma((groups * tiles,)),
            pltpu.SemaphoreType.REGULAR((2,)),
        ],
        compiler_params=pltpu.CompilerParams(
            collective_id=0, has_side_effects=True, vmem_limit_bytes=48 << 20
        ),
        name="align",
    )(*[pltpu.with_memory_space_constraint(a, pltpu.HBM) for a in (patches, tab, nodes, pair_flags.T)])


def solution(mesh):
    placed = (P("sec", "tile", None, None, None), P("sec", None), P(None, "sec", "tile", None))
    return jax.shard_map(
        shards,
        mesh=mesh,
        in_specs=placed,
        out_specs=(P(None, "sec", "tile", None), P(None, "sec", None, "tile", None)),
        check_vma=False,
    )
```

```python
import functools
import math

import jax
import jax.numpy as jnp
import numpy as np
from jax import lax
from jax.experimental import pallas as pl
from jax.experimental.pallas import tpu as pltpu
from jax.sharding import PartitionSpec as P

SWEEPS = 8
STEP_SIZE = 0.08
EPSILON = 1e-06
LANES = 128
TILE = 8
MESH = pl.DeviceIdType.MESH


def tables(n):
    h = n // 2
    k = np.arange(n)
    phase = (k[:, None] * k[None, :] % n) * (2.0 * math.pi / n)
    c = np.asarray(np.cos(phase), np.float32).astype(jnp.bfloat16).astype(np.float32)
    s = np.asarray(np.sin(phase), np.float32).astype(jnp.bfloat16).astype(np.float32)
    part = h + TILE
    first = np.zeros((2 * part, 2 * n), np.float32)
    first[: h + 1, :n] = c[: h + 1]
    first[part : part + h, :n] = s[:h]
    second = np.concatenate([np.concatenate([c, -s], 1), np.concatenate([-s, -c], 1)], 0)
    inverse = np.concatenate([np.concatenate([c, s], 1), np.concatenate([-s, c], 1)], 0)
    order = (np.arange(n) - h) % n
    last = np.zeros((n, 2 * n), np.float32)
    last[:, 0] = c[order, 0]
    last[:, 1:h] = 2.0 * c[order, 1:h]
    last[:, h] = c[order, h]
    last[:, h + 1 : n] = -2.0 * s[order, 1:h]
    last *= 1.0 / float(n) ** 3
    return np.concatenate([first, second, inverse, last], 0).astype(jnp.bfloat16)


def open_tables(tab, n):
    part = n // 2 + TILE
    first = tab[: 2 * part, :n]
    second = tab[2 * part : 2 * part + 2 * n]
    inverse = tab[2 * part + 2 * n : 2 * part + 4 * n]
    last = tab[2 * part + 4 * n :, :n]
    return (first, second), (inverse, last)


def spectra(x, first, second, put):
    cols, n = x.shape[0], x.shape[-1]
    part = n // 2 + TILE
    lines = []
    for c in range(0, cols, 2):
        y = jnp.dot(
            first, jnp.concatenate([x[c], x[c + 1]], axis=1), preferred_element_type=jnp.float32
        )
        for d in (0, 1):
            mine = y[:, d * n : (d + 1) * n]
            lines.append(jnp.concatenate([mine[:part], mine[part:]], axis=1))
    lines = jnp.concatenate(lines, axis=0).astype(jnp.bfloat16)
    spec = jnp.dot(lines, second, preferred_element_type=jnp.float32)
    for c in range(cols):
        mine = spec[c * part : (c + 1) * part]
        put(c, mine[:, :n], mine[:, n:])


def pairs(get_a, get_b, cols, n, inverse, last, put):
    h = n // 2
    part = h + TILE
    crosses = []
    for c in range(cols):
        a, b = get_a(c), get_b(c)
        ar, ai, br, bi = a[:part], a[part:], b[:part], b[part:]
        real = ar * br + ai * bi
        imag = ar * bi - ai * br
        real_top = real[:TILE] - imag[h:]
        imag_top = imag[:TILE] + real[h:]
        real = jnp.concatenate([real_top, real[TILE:h]], axis=0).astype(jnp.bfloat16)
        imag = jnp.concatenate([imag_top, imag[TILE:h]], axis=0).astype(jnp.bfloat16)
        crosses.append(jnp.concatenate([real, imag], axis=1))
    back = jnp.dot(
        jnp.concatenate(crosses, axis=0), inverse, preferred_element_type=jnp.float32
    ).astype(jnp.bfloat16)
    place = lax.broadcasted_iota(jnp.int32, (TILE, 1), 0).astype(jnp.float32) + float(h)
    for c in range(0, cols, 2):
        sides = []
        for d in (c, c + 1):
            mine = back[d * h : (d + 1) * h]
            sides.append(jnp.concatenate([mine[:, :n], mine[:, n:]], axis=0))
        corr = jnp.dot(last, jnp.concatenate(sides, axis=1), preferred_element_type=jnp.float32)
        power = corr * corr
        total = power[:TILE]
        ramp = total
        for t in range(1, n // TILE):
            total = total + power[t * TILE : (t + 1) * TILE]
            ramp = ramp + total
        shifted = place * total - float(TILE) * ramp
        total = jnp.sum(total, axis=0, keepdims=True)
        shifted = jnp.sum(shifted, axis=0, keepdims=True)
        for d in (0, 1):
            put(c + d, shifted[:, d * n : (d + 1) * n], total[:, d * n : (d + 1) * n])


def left_share(boundary, groups, units):
    return units * (groups - 1 - boundary) // groups


def late_cells(groups, local, reach, heap, window):
    units = reach * heap
    halves = 2 * units
    cells = []
    for g in range(groups):
        near = left_share(g, groups, halves) if g < groups - 1 else 0
        before = left_share(g - 1, groups, halves) if g else halves
        right = [("right", k) for k in range((near + 1) // 2)]
        left = [("left", k) for k in range((halves - before + 1) // 2)]
        order = (right + left) if g % 2 else (left + right)
        mine = {}
        for side, k in order[-window:]:
            if side == "right":
                b, h = k // heap, k % heap
                items = [(a, b) for a in range(reach - b)]
            else:
                a, h = k // heap, heap - 1 - k % heap
                items = [(a, b) for b in range((before // 2 + heap - 1 - h) // heap, reach - a)]
            for a, b in items:
                section = (g if side == "right" else g - 1) * local + local - 1 - a
                for part in (0, 1):
                    cut = near if side == "right" else before
                    if cut % 2 and b * heap + h == cut // 2 and part == (side == "right"):
                        continue
                    key = (a + b, 2 * h + part)
                    if key in mine:
                        return None
                    mine[key] = section
        cells.append(mine)
    return cells


def kernel(
    sizes, patches, tab_in, nodes_in, flags_in, moved, shown,
    tab, x, nodes, flags, from_right, from_left, spec, halo, stats, slots, late, lates, field, weight,
    tab_sem, small_sem, own_sem, left_send, left_recv, right_send, right_recv, send, recv, chain,
    pair_sem, even_send, even_recv, tile_send, tile_recv,
):
    groups, tiles, local, reach, rows, cols, n, width, window, cells = sizes
    half = LANES // 2
    part = n // 2 + TILE
    span = rows * cols
    parts = cols // width
    heap = rows * parts
    units = reach * heap
    sec = lax.axis_index("sec")
    tile = lax.axis_index("tile")
    me = sec * tiles + tile
    count = groups * tiles

    def place(index):
        return (index // tiles, index % tiles)

    lates[...] = jnp.zeros_like(lates)
    barrier = pltpu.get_barrier_semaphore()

    for d in range(1, tiles):
        pl.semaphore_signal(
            barrier, inc=1, device_id=(sec, (tile + d) % tiles), device_id_type=MESH
        )

    @pl.when(sec > 0)
    def _():
        pl.semaphore_signal(barrier, inc=1, device_id=(sec - 1, tile), device_id_type=MESH)

    @pl.when(sec < groups - 1)
    def _():
        pl.semaphore_signal(barrier, inc=1, device_id=(sec + 1, tile), device_id_type=MESH)

    tab_copy = pltpu.make_async_copy(tab_in, tab, tab_sem)
    tab_copy.start()

    def own_copy(s):
        return pltpu.make_async_copy(patches.at[s], x.at[s], own_sem.at[s])

    for s in range(local):
        own_copy(s).start()
    node_copy = pltpu.make_async_copy(nodes_in, nodes, small_sem.at[0])
    flag_copy = pltpu.make_async_copy(flags_in, flags, small_sem.at[1])
    node_copy.start()
    flag_copy.start()

    halves = 2 * units
    has_left = (sec + groups - 1) // groups
    has_right = 1 - (sec + 1) // groups
    near = left_share(sec, groups, halves)
    before = left_share(sec - 1, groups, halves)
    sent_left = has_left * ((before + 1) // 2)
    sent_right = has_right * ((halves - near + 1) // 2)
    got_right = has_right * ((near + 1) // 2)
    got_left = has_left * ((halves - before + 1) // 2)
    odd_near, odd_before = near % 2, before % 2

    def spot(h):
        return h // parts, (h % parts) * width

    def copy_left(k, size):
        row, col = spot(k % heap)
        return pltpu.make_async_remote_copy(
            src_ref=patches.at[k // heap, row, pl.ds(col, size)],
            dst_ref=from_right.at[k, pl.ds(0, size)],
            send_sem=left_send.at[k],
            recv_sem=left_recv.at[k],
            device_id=(sec - 1, tile),
            device_id_type=MESH,
        )

    def copy_right(k, size):
        row, col = spot(heap - 1 - k % heap)
        rest = width - size
        return pltpu.make_async_remote_copy(
            src_ref=patches.at[local - 1 - k // heap, row, pl.ds(col + rest, size)],
            dst_ref=from_left.at[k, pl.ds(rest, size)],
            send_sem=right_send.at[k],
            recv_sem=right_recv.at[k],
            device_id=(sec + 1, tile),
            device_id_type=MESH,
        )

    def each(copy, act, k, count, odd, also=True):
        part_unit = (odd == 1) & (k == count - 1) & also

        @pl.when((k >= 0) & (k < count - odd) & also)
        def _():
            act(copy(k, width))

        @pl.when(part_unit)
        def _():
            act(copy(k, width // 2))

    stats[...] = jnp.zeros_like(stats)
    pl.semaphore_wait(barrier, tiles - 1 + has_left + has_right)

    begin = lambda copy: copy.start()
    odd_sec = sec % 2
    hold_left = 2 * odd_sec
    hold_right = 2 - hold_left

    def launch(k, carry):
        each(copy_left, begin, k, sent_left, odd_before, k < sent_left - hold_left)
        each(copy_right, begin, k, sent_right, odd_near, k < sent_right - hold_right)
        return carry

    def launch_held(k, carry):
        each(copy_left, begin, k, sent_left, odd_before, k >= sent_left - hold_left)
        each(copy_right, begin, k, sent_right, odd_near, k >= sent_right - hold_right)
        return carry

    def tell():
        @pl.when(sec > 0)
        def _():
            pl.semaphore_signal(chain.at[1], inc=1, device_id=(sec - 1, tile), device_id_type=MESH)

        @pl.when(sec < groups - 1)
        def _():
            pl.semaphore_signal(chain.at[0], inc=1, device_id=(sec + 1, tile), device_id_type=MESH)

    rounds = groups - 2

    def relay(s, carry):
        @pl.when((s < rounds) & (sec > 0))
        def _():
            pl.semaphore_wait(chain.at[0], 1)

        @pl.when((s < rounds) & (sec < groups - 1))
        def _():
            pl.semaphore_wait(chain.at[1], 1)

        @pl.when(s + 1 < rounds)
        def _():
            tell()

        return carry

    lax.fori_loop(0, units, launch, 0)
    if rounds > 0:
        tell()

    tab_copy.wait()
    forward, inverse = open_tables(tab, n)

    def keep(index, offset, base, low=None, high=None, fresh=False):
        index = jnp.where(fresh, local + reach, index)

        def put(c, shifted, total):
            valid = low if c < width // 2 else high
            if valid is not None:
                shifted = jnp.where(valid, shifted, 0.0)
                total = jnp.where(valid, total, 0.0)
            at = (offset - 1) * span + base + c
            stats[index, pl.ds(at, 1), :] = shifted
            stats[index, pl.ds(half + at, 1), :] = total

        return put

    def own(s, carry):
        own_copy(s).wait()
        for row in range(rows):

            def put(c, real, imag):
                spec[s, row, c, :part] = real
                spec[s, row, c, part:] = imag

            spectra(x.at[s, row], *forward, put)

        def body(offset, carry):
            for row in range(rows):
                pairs(
                    lambda c: spec[s - offset, row, c],
                    lambda c: spec[s, row, c],
                    cols, n, *inverse, keep(s - offset, offset, row * cols),
                )
            return carry

        lax.fori_loop(1, jnp.minimum(s, reach) + 1, body, 0)
        return relay(s, carry)

    lax.fori_loop(0, local, own, 0)
    lax.fori_loop(local, rounds, relay, 0)

    area = float(n * n)
    mine = tile * groups + sec

    def ratios(index):
        sub = lax.broadcasted_iota(jnp.int32, (TILE, n), 0)
        lane = lax.broadcasted_iota(jnp.int32, (TILE, n), 1)
        shift = jnp.where(lane < n // 2, lane, lane - n).astype(jnp.float32)
        weigh = jnp.where(sub == 0, 1.0, jnp.where(sub == 1, shift, 0.0))
        red = lax.dot_general(
            weigh,
            stats[index],
            (((1,), (1,)), ((), ())),
            precision=lax.Precision.HIGHEST,
            preferred_element_type=jnp.float32,
        )
        above, along = red[0:1], red[1:2]
        low = lax.broadcasted_iota(jnp.int32, (1, LANES), 1) < half
        total = jnp.where(low, pltpu.roll(above, half, 1), above) / area + EPSILON
        return jnp.where(low, above, along) / area / total

    def pair_copy():
        return pltpu.make_async_remote_copy(
            src_ref=slots.at[mine],
            dst_ref=slots.at[mine],
            send_sem=pair_sem.at[0],
            recv_sem=pair_sem.at[1],
            device_id=(sec + 1 - 2 * odd_sec, tile),
            device_id_type=MESH,
        )

    def even_copy(pair, other):
        both = pl.ds(tile * groups + 2 * pair, 2)
        return pltpu.make_async_remote_copy(
            src_ref=slots.at[both],
            dst_ref=slots.at[both],
            send_sem=even_send.at[other],
            recv_sem=even_recv.at[pair],
            device_id=(2 * other + odd_sec, tile),
            device_id_type=MESH,
        )

    def tile_copy(column, other):
        whole = pl.ds(column * groups, groups)
        return pltpu.make_async_remote_copy(
            src_ref=slots.at[whole],
            dst_ref=slots.at[whole],
            send_sem=tile_send.at[other],
            recv_sem=tile_recv.at[column],
            device_id=(sec, other),
            device_id_type=MESH,
        )

    def evens(act):
        def visit(d, carry):
            act((sec // 2 + d) % (groups // 2))
            return carry

        lax.fori_loop(1, groups // 2, visit, 0)

    def columns(act):
        def visit(d, carry):
            act((tile + d) % tiles)
            return carry

        lax.fori_loop(1, tiles, visit, 0)

    def publish():
        node_copy.wait()
        flag_copy.wait()
        slots[mine] = jnp.zeros(slots.shape[1:], jnp.float32)
        for index in range(local + reach):
            at = index if index < local else 2 * local + reach - index
            slots[mine, at : at + 1] = ratios(index)
        for comp in range(2):
            for row in range(rows):
                at = comp * half + reach * span + row * cols
                slots[mine, :local, at : at + cols] = nodes[comp, :, row, :]
        for v in range(reach):
            slots[mine, local : local + 1, v * local : (v + 1) * local] = flags[v : v + 1, :].astype(
                jnp.float32
            )
        pair_copy().start()
        lax.fori_loop(0, units, launch_held, 0)

    def spread_pairs():
        pair_copy().wait()
        evens(lambda other: even_copy(sec // 2, other).start())

    def spread_columns():
        evens(lambda other: even_copy(other, other).wait_recv())
        evens(lambda other: even_copy(sec // 2, other).wait_send())
        columns(lambda other: tile_copy(tile, other).start())

    stages = (publish, spread_pairs, spread_columns)

    def put_halo(c, real, imag):
        halo[c, :part] = real
        halo[c, part:] = imag

    got = got_right + got_left

    def far(k, carry):
        fresh = k >= got - window
        for number, stage in enumerate(stages[:window]):
            pl.when(k == got - window + number)(stage)

        u = k - odd_sec * got_right
        k = k - (1 - odd_sec) * got_left

        @pl.when((k >= 0) & (k < got_right))
        def _():
            each(copy_left, lambda copy: copy.wait_recv(), k, got_right, odd_near)
            spectra(from_right.at[k], *forward, put_halo)
            b, h = k // heap, k % heap
            row, col = spot(h)
            whole = (odd_near == 0) | (k < got_right - 1)

            def body(a, carry):
                pairs(
                    lambda c: spec[local - 1 - a, row, col + c],
                    lambda c: halo[c],
                    width, n, *inverse, keep(local - 1 - a, a + b + 1, h * width, None, whole, fresh),
                )
                return carry

            lax.fori_loop(0, reach - b, body, 0)

        @pl.when((u >= 0) & (u < got_left))
        def _():
            each(copy_right, lambda copy: copy.wait_recv(), u, got_left, odd_before)
            spectra(from_left.at[u], *forward, put_halo)
            a, h = u // heap, heap - 1 - u % heap
            row, col = spot(h)
            first = (before // 2 + heap - 1 - h) // heap

            def body(b, carry):
                whole = (odd_before == 0) | (b * heap + h > before // 2)
                pairs(
                    lambda c: halo[c],
                    lambda c: spec[b, row, col + c],
                    width, n, *inverse, keep(local + a, a + b + 1, h * width, whole, None, fresh),
                )
                return carry

            lax.fori_loop(first, reach - a, body, 0)

        return carry

    lax.fori_loop(0, got, far, 0)

    for stage in stages[window:]:
        stage()
    late[...] = ratios(local + reach)

    def copy(source, peer):
        return pltpu.make_async_remote_copy(
            src_ref=late,
            dst_ref=lates.at[source % tiles * groups + source // tiles],
            send_sem=send.at[peer],
            recv_sem=recv.at[source],
            device_id=place(peer),
            device_id_type=MESH,
        )

    span_of = 2 * min(groups - 1, -(-SWEEPS * reach // local)) + 1
    others = span_of * tiles

    def peers(act):
        def visit(d, carry):
            to = sec + d // tiles - span_of // 2
            peer = to * tiles + d % tiles

            @pl.when((to >= 0) & (to < groups) & (peer != me))
            def _():
                act(peer)

            return carry

        lax.fori_loop(0, others, visit, 0, unroll=others <= 64)

    peers(lambda peer: copy(me, peer).start())
    lates[mine] = late[...]
    columns(lambda other: tile_copy(other, other).wait_recv())
    columns(lambda other: tile_copy(tile, other).wait_send())

    def sent(k, carry):
        done = lambda copy: copy.wait_send()
        each(copy_left, done, k, sent_left, odd_before)
        each(copy_right, done, k, sent_right, odd_near)
        return carry

    lax.fori_loop(0, units, sent, 0)

    lane = lax.broadcasted_iota(jnp.int32, (TILE, LANES), 1)
    sub = lax.broadcasted_iota(jnp.int32, (TILE, LANES), 0)
    owner = lane % half // span
    total = groups * local
    for g in range(groups):
        flat = jnp.broadcast_to(slots[g, local : local + 1], (TILE, LANES))
        for v in range(reach):
            w = jnp.sum(jnp.where(lane == v * local + sub, flat, 0.0), axis=1, keepdims=True)
            w = jnp.broadcast_to(w, (TILE, LANES))
            w = jnp.where(g * local + sub + v + 1 < total, w, 0.0)
            weight[v, g * local : (g + 1) * local, :] = w[:local]
        blocks = []
        for t in range(tiles):
            block = slots[t * groups + g, :local]
            if g < groups - 1:
                add = slots[t * groups + g + 1, local + 1 :]
                block = jnp.concatenate([block[: local - reach], block[local - reach :] + add], axis=0)
            blocks.append(jnp.concatenate([block, jnp.zeros((TILE - local, LANES), jnp.float32)], axis=0))
        for v in range(reach + 1):
            value = jnp.zeros((TILE, LANES), jnp.float32)
            for t in range(tiles):
                moved_to = blocks[t]
                if t != v:
                    moved_to = pltpu.roll(moved_to, (t - v) * span % LANES, 1)
                value = jnp.where(owner == t, moved_to, value)
            value = value[:local]
            if v < reach:
                value = value * weight[v, g * local : (g + 1) * local, :]
            field[v, g * local : (g + 1) * local, :] = value

    def finish(peer):
        copy(peer, peer).wait_recv()
        copy(me, peer).wait_send()

    peers(finish)
    slot = lax.broadcasted_iota(jnp.int32, (1, LANES), 1) % span // (width // 2)
    column = lax.broadcasted_iota(jnp.int32, (groups, LANES), 1) % half // span
    blocks = [lates[pl.ds(t * groups, groups), 0, :] for t in range(tiles)]
    for v in range(reach):
        value = jnp.zeros((groups, LANES), jnp.float32)
        for t in range(tiles):
            block = blocks[t]
            if t != v:
                block = pltpu.roll(block, (t - v) * span % LANES, 1)
            value = jnp.where(column == t, block, value)
        for g in range(groups):
            found = {}
            for (o, part), section in sorted(cells[g].items()):
                if o == v:
                    found.setdefault(section, []).append(part)
            for section, places in sorted(found.items()):
                line = value[g : g + 1]
                if len(found) > 1:
                    inside = slot == places[0]
                    for part in places[1:]:
                        inside = inside | (slot == part)
                    line = jnp.where(inside, line, 0.0)
                here = slice(section, section + 1)
                field[v, here, :] = field[v, here, :] + line * weight[v, here, :]

    grid_rows = tiles * rows
    at = lax.broadcasted_iota(jnp.int32, (total, LANES), 1) % half
    across = at % cols
    down = at // cols
    one = lambda mask: mask.astype(jnp.float32)
    left, right = one(across > 0), one(across < cols - 1)
    up, below = one(down > 0), one(down < grid_rows - 1)

    def sweep(_, u):
        plane = (
            up * (pltpu.roll(u, cols, 1) - u)
            + below * (pltpu.roll(u, LANES - cols, 1) - u)
            + left * (pltpu.roll(u, 1, 1) - u)
            + right * (pltpu.roll(u, LANES - 1, 1) - u)
        )
        spring = jnp.zeros_like(u)
        for v in range(reach):
            o = v + 1
            r = weight[v] * (pltpu.roll(u, total - o, 0) - u) - field[v]
            spring = spring + r - pltpu.roll(r, o, 0)
        return u + STEP_SIZE * (plane + spring)

    field[reach] = lax.fori_loop(0, SWEEPS, sweep, field[reach])
    back = (LANES - tile * span) % LANES
    for v in range(reach + 1):
        mine = pltpu.roll(field[v, pl.ds(sec * local, local), :], back, 1)
        for comp in range(2):
            for row in range(rows):
                at = comp * half + row * cols
                piece = mine[:, at : at + cols]
                if v < reach:
                    shown[comp, :, v, row, :] = piece
                else:
                    moved[comp, :, row, :] = piece


def shards(patches, pair_flags, nodes):
    local, rows, cols, n = patches.shape[:4]
    reach = pair_flags.shape[1]
    groups, tiles = lax.axis_size("sec"), lax.axis_size("tile")
    part = n // 2 + TILE
    width = cols // 2
    units = reach * rows * cols // width
    tab = jnp.asarray(tables(n))
    heap = units // reach
    window = 3
    while window > 1 and late_cells(groups, local, reach, heap, window) is None:
        window -= 1
    cells = late_cells(groups, local, reach, heap, window)
    sizes = (groups, tiles, local, reach, rows, cols, n, width, window, cells)
    hbm = pl.BlockSpec(memory_space=pltpu.HBM)
    vmem = pl.BlockSpec(memory_space=pltpu.VMEM)
    dma = pltpu.SemaphoreType.DMA
    return pl.pallas_call(
        functools.partial(kernel, sizes),
        in_specs=[hbm] * 4,
        out_specs=[vmem] * 2,
        out_shape=[
            jax.ShapeDtypeStruct((2, local, rows, cols), jnp.float32),
            jax.ShapeDtypeStruct((2, local, reach, rows, cols), jnp.float32),
        ],
        scratch_shapes=[
            pltpu.VMEM(tab.shape, jnp.bfloat16),
            pltpu.VMEM((local, rows, cols, n, n), jnp.bfloat16),
            pltpu.VMEM(nodes.shape, jnp.float32),
            pltpu.VMEM((reach, local), jnp.int32),
            pltpu.VMEM((units, width, n, n), jnp.bfloat16),
            pltpu.VMEM((units, width, n, n), jnp.bfloat16),
            pltpu.VMEM((local, rows, cols, 2 * part, n), jnp.float32),
            pltpu.VMEM((width, 2 * part, n), jnp.float32),
            pltpu.VMEM((local + reach + 1, LANES, LANES), jnp.float32),
            pltpu.VMEM((groups * tiles, local + reach + 1, LANES), jnp.float32),
            pltpu.VMEM((1, LANES), jnp.float32),
            pltpu.VMEM((groups * tiles, 1, LANES), jnp.float32),
            pltpu.VMEM((reach + 1, groups * local, LANES), jnp.float32),
            pltpu.VMEM((reach, groups * local, LANES), jnp.float32),
            dma,
            dma((2,)),
            dma((local,)),
            dma((units,)),
            dma((units,)),
            dma((units,)),
            dma((units,)),
            dma((groups * tiles,)),
            dma((groups * tiles,)),
            pltpu.SemaphoreType.REGULAR((2,)),
            dma((2,)),
            dma((groups // 2,)),
            dma((groups // 2,)),
            dma((tiles,)),
            dma((tiles,)),
        ],
        compiler_params=pltpu.CompilerParams(
            collective_id=0, has_side_effects=True, vmem_limit_bytes=48 << 20
        ),
        name="align",
    )(*[pltpu.with_memory_space_constraint(a, pltpu.HBM) for a in (patches, tab, nodes, pair_flags.T)])


def solution(mesh):
    placed = (P("sec", "tile", None, None, None), P("sec", None), P(None, "sec", "tile", None))
    return jax.shard_map(
        shards,
        mesh=mesh,
        in_specs=placed,
        out_specs=(P(None, "sec", "tile", None), P(None, "sec", None, "tile", None)),
        check_vma=False,
    )
```

```python
import functools
import math

import jax
import jax.numpy as jnp
import numpy as np
from jax import lax
from jax.experimental import pallas as pl
from jax.experimental.pallas import tpu as pltpu
from jax.sharding import PartitionSpec as P

SWEEPS = 8
STEP_SIZE = 0.08
EPSILON = 1e-06
LANES = 128
TILE = 8
MESH = pl.DeviceIdType.MESH


def tables(n):
    h = n // 2
    k = np.arange(n)
    phase = (k[:, None] * k[None, :] % n) * (2.0 * math.pi / n)
    c = np.asarray(np.cos(phase), np.float32).astype(jnp.bfloat16).astype(np.float32)
    s = np.asarray(np.sin(phase), np.float32).astype(jnp.bfloat16).astype(np.float32)
    part = h + TILE
    first = np.zeros((2 * part, 2 * n), np.float32)
    first[: h + 1, :n] = c[: h + 1]
    first[part : part + h, :n] = s[:h]
    second = np.concatenate([np.concatenate([c, -s], 1), np.concatenate([-s, -c], 1)], 0)
    inverse = np.concatenate([np.concatenate([c, s], 1), np.concatenate([-s, c], 1)], 0)
    order = (np.arange(n) - h) % n
    last = np.zeros((n, 2 * n), np.float32)
    last[:, 0] = c[order, 0]
    last[:, 1:h] = 2.0 * c[order, 1:h]
    last[:, h] = c[order, h]
    last[:, h + 1 : n] = -2.0 * s[order, 1:h]
    last *= 1.0 / float(n) ** 3
    return np.concatenate([first, second, inverse, last], 0).astype(jnp.bfloat16)


def open_tables(tab, n):
    part = n // 2 + TILE
    first = tab[: 2 * part, :n]
    second = tab[2 * part : 2 * part + 2 * n]
    inverse = tab[2 * part + 2 * n : 2 * part + 4 * n]
    last = tab[2 * part + 4 * n :, :n]
    return (first, second), (inverse, last)


def spectra(x, first, second, put):
    cols, n = x.shape[0], x.shape[-1]
    part = n // 2 + TILE
    lines = []
    for c in range(0, cols, 2):
        y = jnp.dot(
            first, jnp.concatenate([x[c], x[c + 1]], axis=1), preferred_element_type=jnp.float32
        )
        for d in (0, 1):
            mine = y[:, d * n : (d + 1) * n]
            lines.append(jnp.concatenate([mine[:part], mine[part:]], axis=1))
    lines = jnp.concatenate(lines, axis=0).astype(jnp.bfloat16)
    spec = jnp.dot(lines, second, preferred_element_type=jnp.float32)
    for c in range(cols):
        mine = spec[c * part : (c + 1) * part]
        put(c, mine[:, :n], mine[:, n:])


def pairs(get_a, get_b, cols, n, inverse, last, put):
    h = n // 2
    part = h + TILE
    crosses = []
    for c in range(cols):
        a, b = get_a(c), get_b(c)
        ar, ai, br, bi = a[:part], a[part:], b[:part], b[part:]
        real = ar * br + ai * bi
        imag = ar * bi - ai * br
        real_top = real[:TILE] - imag[h:]
        imag_top = imag[:TILE] + real[h:]
        real = jnp.concatenate([real_top, real[TILE:h]], axis=0).astype(jnp.bfloat16)
        imag = jnp.concatenate([imag_top, imag[TILE:h]], axis=0).astype(jnp.bfloat16)
        crosses.append(jnp.concatenate([real, imag], axis=1))
    back = jnp.dot(
        jnp.concatenate(crosses, axis=0), inverse, preferred_element_type=jnp.float32
    ).astype(jnp.bfloat16)
    place = lax.broadcasted_iota(jnp.int32, (TILE, 1), 0).astype(jnp.float32) + float(h)
    for c in range(0, cols, 2):
        sides = []
        for d in (c, c + 1):
            mine = back[d * h : (d + 1) * h]
            sides.append(jnp.concatenate([mine[:, :n], mine[:, n:]], axis=0))
        corr = jnp.dot(last, jnp.concatenate(sides, axis=1), preferred_element_type=jnp.float32)
        power = corr * corr
        total = power[:TILE]
        ramp = total
        for t in range(1, n // TILE):
            total = total + power[t * TILE : (t + 1) * TILE]
            ramp = ramp + total
        shifted = place * total - float(TILE) * ramp
        total = jnp.sum(total, axis=0, keepdims=True)
        shifted = jnp.sum(shifted, axis=0, keepdims=True)
        for d in (0, 1):
            put(c + d, shifted[:, d * n : (d + 1) * n], total[:, d * n : (d + 1) * n])


def left_share(boundary, groups, units):
    return units * (groups - 1 - boundary) // groups


def late_cells(groups, local, reach, heap, window):
    units = reach * heap
    halves = 2 * units
    cells = []
    for g in range(groups):
        near = left_share(g, groups, halves) if g < groups - 1 else 0
        before = left_share(g - 1, groups, halves) if g else halves
        right = [("right", k) for k in range((near + 1) // 2)]
        left = [("left", k) for k in range((halves - before + 1) // 2)]
        order = (right + left) if g % 2 else (left + right)
        mine = {}
        for side, k in order[-window:]:
            if side == "right":
                b, h = k // heap, k % heap
                items = [(a, b) for a in range(reach - b)]
            else:
                a, h = k // heap, heap - 1 - k % heap
                items = [(a, b) for b in range((before // 2 + heap - 1 - h) // heap, reach - a)]
            for a, b in items:
                section = (g if side == "right" else g - 1) * local + local - 1 - a
                for part in (0, 1):
                    cut = near if side == "right" else before
                    if cut % 2 and b * heap + h == cut // 2 and part == (side == "right"):
                        continue
                    key = (a + b, 2 * h + part)
                    if key in mine:
                        return None
                    mine[key] = section
        cells.append(mine)
    return cells


def kernel(
    sizes, patches, tab_in, nodes_in, flags_in, moved, shown,
    tab, x, nodes, flags, from_right, from_left, spec, halo, stats, slots, combs, late, lates, field, weight,
    tab_sem, small_sem, own_sem, left_send, left_recv, right_send, right_recv, send, recv, chain,
    group_send, group_recv, tile_send, tile_recv,
):
    groups, tiles, local, reach, rows, cols, n, width, window, cells = sizes
    half = LANES // 2
    part = n // 2 + TILE
    span = rows * cols
    parts = cols // width
    heap = rows * parts
    units = reach * heap
    sec = lax.axis_index("sec")
    tile = lax.axis_index("tile")

    lates[...] = jnp.zeros_like(lates)
    barrier = pltpu.get_barrier_semaphore()

    for d in range(1, tiles):
        pl.semaphore_signal(
            barrier, inc=1, device_id=(sec, (tile + d) % tiles), device_id_type=MESH
        )

    @pl.when(sec > 0)
    def _():
        pl.semaphore_signal(barrier, inc=1, device_id=(sec - 1, tile), device_id_type=MESH)

    @pl.when(sec < groups - 1)
    def _():
        pl.semaphore_signal(barrier, inc=1, device_id=(sec + 1, tile), device_id_type=MESH)

    tab_copy = pltpu.make_async_copy(tab_in, tab, tab_sem)
    tab_copy.start()

    def own_copy(s):
        return pltpu.make_async_copy(patches.at[s], x.at[s], own_sem.at[s])

    for s in range(local):
        own_copy(s).start()
    node_copy = pltpu.make_async_copy(nodes_in, nodes, small_sem.at[0])
    flag_copy = pltpu.make_async_copy(flags_in, flags, small_sem.at[1])
    node_copy.start()
    flag_copy.start()

    halves = 2 * units
    has_left = (sec + groups - 1) // groups
    has_right = 1 - (sec + 1) // groups
    near = left_share(sec, groups, halves)
    before = left_share(sec - 1, groups, halves)
    sent_left = has_left * ((before + 1) // 2)
    sent_right = has_right * ((halves - near + 1) // 2)
    got_right = has_right * ((near + 1) // 2)
    got_left = has_left * ((halves - before + 1) // 2)
    odd_near, odd_before = near % 2, before % 2

    def spot(h):
        return h // parts, (h % parts) * width

    def copy_left(k, size):
        row, col = spot(k % heap)
        return pltpu.make_async_remote_copy(
            src_ref=patches.at[k // heap, row, pl.ds(col, size)],
            dst_ref=from_right.at[k, pl.ds(0, size)],
            send_sem=left_send.at[k],
            recv_sem=left_recv.at[k],
            device_id=(sec - 1, tile),
            device_id_type=MESH,
        )

    def copy_right(k, size):
        row, col = spot(heap - 1 - k % heap)
        rest = width - size
        return pltpu.make_async_remote_copy(
            src_ref=patches.at[local - 1 - k // heap, row, pl.ds(col + rest, size)],
            dst_ref=from_left.at[k, pl.ds(rest, size)],
            send_sem=right_send.at[k],
            recv_sem=right_recv.at[k],
            device_id=(sec + 1, tile),
            device_id_type=MESH,
        )

    def each(copy, act, k, count, odd, also=True):
        part_unit = (odd == 1) & (k == count - 1) & also

        @pl.when((k >= 0) & (k < count - odd) & also)
        def _():
            act(copy(k, width))

        @pl.when(part_unit)
        def _():
            act(copy(k, width // 2))

    stats[...] = jnp.zeros_like(stats)
    pl.semaphore_wait(barrier, tiles - 1 + has_left + has_right)

    begin = lambda copy: copy.start()
    odd_sec = sec % 2
    hold_left = 1 * odd_sec
    hold_right = 1 - hold_left

    def launch(k, carry):
        each(copy_left, begin, k, sent_left, odd_before, k < sent_left - hold_left)
        each(copy_right, begin, k, sent_right, odd_near, k < sent_right - hold_right)
        return carry

    def launch_held(k, carry):
        each(copy_left, begin, k, sent_left, odd_before, k >= sent_left - hold_left)
        each(copy_right, begin, k, sent_right, odd_near, k >= sent_right - hold_right)
        return carry

    def tell():
        @pl.when(sec > 0)
        def _():
            pl.semaphore_signal(chain.at[1], inc=1, device_id=(sec - 1, tile), device_id_type=MESH)

        @pl.when(sec < groups - 1)
        def _():
            pl.semaphore_signal(chain.at[0], inc=1, device_id=(sec + 1, tile), device_id_type=MESH)

    rounds = groups - 2

    def relay(s, carry):
        @pl.when((s < rounds) & (sec > 0))
        def _():
            pl.semaphore_wait(chain.at[0], 1)

        @pl.when((s < rounds) & (sec < groups - 1))
        def _():
            pl.semaphore_wait(chain.at[1], 1)

        @pl.when(s + 1 < rounds)
        def _():
            tell()

        return carry

    lax.fori_loop(0, units, launch, 0)
    if rounds > 0:
        tell()

    tab_copy.wait()
    forward, inverse = open_tables(tab, n)

    def keep(index, offset, base, low=None, high=None, fresh=False):
        index = jnp.where(fresh, local + reach, index)

        def put(c, shifted, total):
            valid = low if c < width // 2 else high
            if valid is not None:
                shifted = jnp.where(valid, shifted, 0.0)
                total = jnp.where(valid, total, 0.0)
            at = (offset - 1) * span + base + c
            stats[index, pl.ds(at, 1), :] = shifted
            stats[index, pl.ds(half + at, 1), :] = total

        return put

    def own(s, carry):
        own_copy(s).wait()
        for row in range(rows):

            def put(c, real, imag):
                spec[s, row, c, :part] = real
                spec[s, row, c, part:] = imag

            spectra(x.at[s, row], *forward, put)

        def body(offset, carry):
            for row in range(rows):
                pairs(
                    lambda c: spec[s - offset, row, c],
                    lambda c: spec[s, row, c],
                    cols, n, *inverse, keep(s - offset, offset, row * cols),
                )
            return carry

        lax.fori_loop(1, jnp.minimum(s, reach) + 1, body, 0)
        return relay(s, carry)

    lax.fori_loop(0, local, own, 0)
    lax.fori_loop(local, rounds, relay, 0)

    area = float(n * n)
    mine = tile * groups + sec

    def ratios(index):
        sub = lax.broadcasted_iota(jnp.int32, (TILE, n), 0)
        lane = lax.broadcasted_iota(jnp.int32, (TILE, n), 1)
        shift = jnp.where(lane < n // 2, lane, lane - n).astype(jnp.float32)
        weigh = jnp.where(sub == 0, 1.0, jnp.where(sub == 1, shift, 0.0))
        red = lax.dot_general(
            weigh,
            stats[index],
            (((1,), (1,)), ((), ())),
            precision=lax.Precision.HIGHEST,
            preferred_element_type=jnp.float32,
        )
        above, along = red[0:1], red[1:2]
        low = lax.broadcasted_iota(jnp.int32, (1, LANES), 1) < half
        total = jnp.where(low, pltpu.roll(above, half, 1), above) / area + EPSILON
        return jnp.where(low, above, along) / area / total

    def group_copy(source, other):
        return pltpu.make_async_remote_copy(
            src_ref=slots.at[source],
            dst_ref=slots.at[source],
            send_sem=group_send.at[other],
            recv_sem=group_recv.at[source],
            device_id=(other, tile),
            device_id_type=MESH,
        )

    def tile_copy(column, other):
        return pltpu.make_async_remote_copy(
            src_ref=combs.at[column],
            dst_ref=combs.at[column],
            send_sem=tile_send.at[other],
            recv_sem=tile_recv.at[column],
            device_id=(sec, other),
            device_id_type=MESH,
        )

    def groups_else(act):
        def visit(d, carry):
            act((sec + d) % groups)
            return carry

        lax.fori_loop(1, groups, visit, 0)

    def columns(act):
        def visit(d, carry):
            act((tile + d) % tiles)
            return carry

        lax.fori_loop(1, tiles, visit, 0)

    def publish():
        node_copy.wait()
        flag_copy.wait()
        slots[sec] = jnp.zeros(slots.shape[1:], jnp.float32)
        for index in range(local + reach):
            at = index if index < local else 2 * local + reach - index
            slots[sec, at : at + 1] = ratios(index)
        for comp in range(2):
            for row in range(rows):
                at = comp * half + reach * span + row * cols
                slots[sec, :local, at : at + cols] = nodes[comp, :, row, :]
        for v in range(reach):
            slots[sec, local : local + 1, v * local : (v + 1) * local] = flags[v : v + 1, :].astype(
                jnp.float32
            )
        groups_else(lambda other: group_copy(sec, other).start())
        lax.fori_loop(0, units, launch_held, 0)

    def spread_columns():
        groups_else(lambda other: group_copy(other, other).wait_recv())
        groups_else(lambda other: group_copy(sec, other).wait_send())
        for g in range(groups):
            block = slots[g, :local]
            if g < groups - 1:
                add = slots[g + 1, local + 1 :]
                block = jnp.concatenate([block[: local - reach], block[local - reach :] + add], axis=0)
            combs[tile, g * local : (g + 1) * local] = block
        columns(lambda other: tile_copy(tile, other).start())


    def put_halo(c, real, imag):
        halo[c, :part] = real
        halo[c, part:] = imag

    got = got_right + got_left

    def far(k, carry):
        fresh = k >= got - window
        pl.when(k == got - window)(publish)
        if window > 1:
            pl.when(k == got - 1)(spread_columns)

        u = k - odd_sec * got_right
        k = k - (1 - odd_sec) * got_left

        done = lambda copy: copy.wait_recv()
        each(copy_left, done, k, got_right, odd_near)
        each(copy_right, done, u, got_left, odd_before)
        from_next = (k >= 0) & (k < got_right)
        from_last = (u >= 0) & (u < got_left)
        next_spot = k % heap
        last_spot = heap - 1 - u % heap
        first = (before // 2 + heap - 1 - last_spot) // heap

        for many in range(1, reach + 1):

            @pl.when(from_next & (reach - k // heap == many))
            def _():
                spectra(from_right.at[k], *forward, put_halo)
                row, col = spot(next_spot)
                whole = (odd_near == 0) | (k < got_right - 1)
                for a in range(many):
                    pairs(
                        lambda c: spec[local - 1 - a, row, col + c],
                        lambda c: halo[c],
                        width, n, *inverse,
                        keep(local - 1 - a, a + reach - many + 1, next_spot * width, None, whole, fresh),
                    )

            @pl.when(from_last & (reach - u // heap - first == many))
            def _():
                spectra(from_left.at[u], *forward, put_halo)
                row, col = spot(last_spot)
                a = u // heap
                for d in range(many):
                    b = first + d
                    whole = (odd_before == 0) | (b * heap + last_spot > before // 2)
                    pairs(
                        lambda c: halo[c],
                        lambda c: spec[b, row, col + c],
                        width, n, *inverse,
                        keep(local + a, a + b + 1, last_spot * width, whole, None, fresh),
                    )

        return carry

    lax.fori_loop(0, got, far, 0)

    if window == 1:
        spread_columns()
    late[...] = ratios(local + reach)

    far_off = min(groups - 1, -(-SWEEPS * reach // local))
    deltas = sorted(range(-far_off, far_off + 1), key=lambda delta: -abs(delta))

    def late_copy(delta, to):
        return pltpu.make_async_remote_copy(
            src_ref=late,
            dst_ref=lates.at[mine],
            send_sem=send.at[delta + far_off],
            recv_sem=recv.at[delta + far_off],
            device_id=(sec + delta, to),
            device_id_type=MESH,
        )

    def late_sum(delta):
        several = lates.at[pl.ds(0, tiles if delta else tiles - 1)]
        return pltpu.make_async_remote_copy(
            src_ref=several,
            dst_ref=several,
            send_sem=send.at[delta + far_off],
            recv_sem=recv.at[delta + far_off],
            device_id=(sec, (tile + 1) % tiles),
            device_id_type=MESH,
        )

    def peers(sign, act):
        for delta in deltas:
            to = sec + sign * delta
            pl.when((to >= 0) & (to < groups))(functools.partial(act, delta))

    def send_late(delta):
        for d in range(0 if delta else 1, tiles):
            late_copy(delta, (tile + d) % tiles).start()

    peers(1, send_late)
    lates[mine] = late[...]

    def sent(k, carry):
        done = lambda copy: copy.wait_send()
        each(copy_left, done, k, sent_left, odd_before)
        each(copy_right, done, k, sent_right, odd_near)
        return carry

    lax.fori_loop(0, units, sent, 0)

    lane = lax.broadcasted_iota(jnp.int32, (TILE, LANES), 1)
    sub = lax.broadcasted_iota(jnp.int32, (TILE, LANES), 0)
    total = groups * local
    for g in range(groups):
        flat = jnp.broadcast_to(slots[g, local : local + 1], (TILE, LANES))
        for v in range(reach):
            w = jnp.sum(jnp.where(lane == v * local + sub, flat, 0.0), axis=1, keepdims=True)
            w = jnp.broadcast_to(w, (TILE, LANES))
            w = jnp.where(g * local + sub + v + 1 < total, w, 0.0)
            weight[v, g * local : (g + 1) * local, :] = w[:local]
    columns(lambda other: tile_copy(other, other).wait_recv())
    owner = lax.broadcasted_iota(jnp.int32, (total, LANES), 1) % half // span
    for v in range(reach + 1):
        value = jnp.zeros((total, LANES), jnp.float32)
        for t in range(tiles):
            block = combs[t]
            if t != v:
                block = pltpu.roll(block, (t - v) * span % LANES, 1)
            value = jnp.where(owner == t, block, value)
        field[v] = value * weight[v] if v < reach else value

    peers(-1, lambda delta: late_sum(delta).wait_recv())
    slot = lax.broadcasted_iota(jnp.int32, (1, LANES), 1) % span // (width // 2)
    column = lax.broadcasted_iota(jnp.int32, (groups, LANES), 1) % half // span
    blocks = [lates[pl.ds(t * groups, groups), 0, :] for t in range(tiles)]
    for v in range(reach):
        value = jnp.zeros((groups, LANES), jnp.float32)
        for t in range(tiles):
            block = blocks[t]
            if t != v:
                block = pltpu.roll(block, (t - v) * span % LANES, 1)
            value = jnp.where(column == t, block, value)
        for g in range(groups):
            found = {}
            for (o, part), section in sorted(cells[g].items()):
                if o == v:
                    found.setdefault(section, []).append(part)
            for section, places in sorted(found.items()):
                line = value[g : g + 1]
                if len(found) > 1:
                    inside = slot == places[0]
                    for part in places[1:]:
                        inside = inside | (slot == part)
                    line = jnp.where(inside, line, 0.0)
                here = slice(section, section + 1)
                field[v, here, :] = field[v, here, :] + line * weight[v, here, :]

    grid_rows = tiles * rows
    at = lax.broadcasted_iota(jnp.int32, (total, LANES), 1) % half
    across = at % cols
    down = at // cols
    one = lambda mask: mask.astype(jnp.float32)
    left, right = one(across > 0), one(across < cols - 1)
    up, below = one(down > 0), one(down < grid_rows - 1)

    def sweep(_, u):
        plane = (
            up * (pltpu.roll(u, cols, 1) - u)
            + below * (pltpu.roll(u, LANES - cols, 1) - u)
            + left * (pltpu.roll(u, 1, 1) - u)
            + right * (pltpu.roll(u, LANES - 1, 1) - u)
        )
        spring = jnp.zeros_like(u)
        for v in range(reach):
            o = v + 1
            r = weight[v] * (pltpu.roll(u, total - o, 0) - u) - field[v]
            spring = spring + r - pltpu.roll(r, o, 0)
        return u + STEP_SIZE * (plane + spring)

    field[reach] = lax.fori_loop(0, SWEEPS, sweep, field[reach])
    back = (LANES - tile * span) % LANES
    for v in range(reach + 1):
        mine = pltpu.roll(field[v, pl.ds(sec * local, local), :], back, 1)
        for comp in range(2):
            for row in range(rows):
                at = comp * half + row * cols
                piece = mine[:, at : at + cols]
                if v < reach:
                    shown[comp, :, v, row, :] = piece
                else:
                    moved[comp, :, row, :] = piece

    columns(lambda other: tile_copy(tile, other).wait_send())
    peers(1, lambda delta: late_sum(delta).wait_send())


def shards(patches, pair_flags, nodes):
    local, rows, cols, n = patches.shape[:4]
    reach = pair_flags.shape[1]
    groups, tiles = lax.axis_size("sec"), lax.axis_size("tile")
    part = n // 2 + TILE
    width = cols // 2
    units = reach * rows * cols // width
    tab = jnp.asarray(tables(n))
    heap = units // reach
    window = 3
    while window > 1 and late_cells(groups, local, reach, heap, window) is None:
        window -= 1
    cells = late_cells(groups, local, reach, heap, window)
    sizes = (groups, tiles, local, reach, rows, cols, n, width, window, cells)
    hbm = pl.BlockSpec(memory_space=pltpu.HBM)
    vmem = pl.BlockSpec(memory_space=pltpu.VMEM)
    dma = pltpu.SemaphoreType.DMA
    return pl.pallas_call(
        functools.partial(kernel, sizes),
        in_specs=[hbm] * 4,
        out_specs=[vmem] * 2,
        out_shape=[
            jax.ShapeDtypeStruct((2, local, rows, cols), jnp.float32),
            jax.ShapeDtypeStruct((2, local, reach, rows, cols), jnp.float32),
        ],
        scratch_shapes=[
            pltpu.VMEM(tab.shape, jnp.bfloat16),
            pltpu.VMEM((local, rows, cols, n, n), jnp.bfloat16),
            pltpu.VMEM(nodes.shape, jnp.float32),
            pltpu.VMEM((reach, local), jnp.int32),
            pltpu.VMEM((units, width, n, n), jnp.bfloat16),
            pltpu.VMEM((units, width, n, n), jnp.bfloat16),
            pltpu.VMEM((local, rows, cols, 2 * part, n), jnp.float32),
            pltpu.VMEM((width, 2 * part, n), jnp.float32),
            pltpu.VMEM((local + reach + 1, LANES, LANES), jnp.float32),
            pltpu.VMEM((groups, local + reach + 1, LANES), jnp.float32),
            pltpu.VMEM((tiles, groups * local, LANES), jnp.float32),
            pltpu.VMEM((1, LANES), jnp.float32),
            pltpu.VMEM((groups * tiles, 1, LANES), jnp.float32),
            pltpu.VMEM((reach + 1, groups * local, LANES), jnp.float32),
            pltpu.VMEM((reach, groups * local, LANES), jnp.float32),
            dma,
            dma((2,)),
            dma((local,)),
            dma((units,)),
            dma((units,)),
            dma((units,)),
            dma((units,)),
            dma((2 * groups,)),
            dma((2 * groups,)),
            pltpu.SemaphoreType.REGULAR((2,)),
            dma((groups,)),
            dma((groups,)),
            dma((tiles,)),
            dma((tiles,)),
        ],
        compiler_params=pltpu.CompilerParams(
            collective_id=0, has_side_effects=True, vmem_limit_bytes=48 << 20
        ),
        name="align",
    )(*[pltpu.with_memory_space_constraint(a, pltpu.HBM) for a in (patches, tab, nodes, pair_flags.T)])


def solution(mesh):
    placed = (P("sec", "tile", None, None, None), P("sec", None), P(None, "sec", "tile", None))
    return jax.shard_map(
        shards,
        mesh=mesh,
        in_specs=placed,
        out_specs=(P(None, "sec", "tile", None), P(None, "sec", None, "tile", None)),
        check_vma=False,
    )
```

```python
import functools
import math

import jax
import jax.numpy as jnp
import numpy as np
from jax import lax
from jax.experimental import pallas as pl
from jax.experimental.pallas import tpu as pltpu
from jax.sharding import PartitionSpec as P

SWEEPS = 8
STEP_SIZE = 0.08
EPSILON = 1e-06
LANES = 128
TILE = 8
MESH = pl.DeviceIdType.MESH


def tables(n):
    h = n // 2
    k = np.arange(n)
    phase = (k[:, None] * k[None, :] % n) * (2.0 * math.pi / n)
    c = np.asarray(np.cos(phase), np.float32).astype(jnp.bfloat16).astype(np.float32)
    s = np.asarray(np.sin(phase), np.float32).astype(jnp.bfloat16).astype(np.float32)
    part = h + TILE
    first = np.zeros((2 * part, 2 * n), np.float32)
    first[: h + 1, :n] = c[: h + 1]
    first[part : part + h, :n] = s[:h]
    second = np.concatenate([np.concatenate([c, -s], 1), np.concatenate([-s, -c], 1)], 0)
    inverse = np.concatenate([np.concatenate([c, s], 1), np.concatenate([-s, c], 1)], 0)
    order = (np.arange(n) - h) % n
    last = np.zeros((n, 2 * n), np.float32)
    last[:, 0] = c[order, 0]
    last[:, 1:h] = 2.0 * c[order, 1:h]
    last[:, h] = c[order, h]
    last[:, h + 1 : n] = -2.0 * s[order, 1:h]
    last *= 1.0 / float(n) ** 3
    return np.concatenate([first, second, inverse, last], 0).astype(jnp.bfloat16)


def open_tables(tab, n):
    part = n // 2 + TILE
    first = tab[: 2 * part, :n]
    second = tab[2 * part : 2 * part + 2 * n]
    inverse = tab[2 * part + 2 * n : 2 * part + 4 * n]
    last = tab[2 * part + 4 * n :, :n]
    return (first, second), (inverse, last)


def spectra(x, first, second, put):
    cols, n = x.shape[0], x.shape[-1]
    part = n // 2 + TILE
    lines = []
    for c in range(0, cols, 2):
        y = jnp.dot(
            first, jnp.concatenate([x[c], x[c + 1]], axis=1), preferred_element_type=jnp.float32
        )
        for d in (0, 1):
            mine = y[:, d * n : (d + 1) * n]
            lines.append(jnp.concatenate([mine[:part], mine[part:]], axis=1))
    lines = jnp.concatenate(lines, axis=0).astype(jnp.bfloat16)
    spec = jnp.dot(lines, second, preferred_element_type=jnp.float32)
    for c in range(cols):
        mine = spec[c * part : (c + 1) * part]
        put(c, mine[:, :n], mine[:, n:])


def pairs(get_a, get_b, cols, n, inverse, last, put):
    h = n // 2
    part = h + TILE
    crosses = []
    for c in range(cols):
        a, b = get_a(c), get_b(c)
        ar, ai, br, bi = a[:part], a[part:], b[:part], b[part:]
        real = ar * br + ai * bi
        imag = ar * bi - ai * br
        real_top = real[:TILE] - imag[h:]
        imag_top = imag[:TILE] + real[h:]
        real = jnp.concatenate([real_top, real[TILE:h]], axis=0).astype(jnp.bfloat16)
        imag = jnp.concatenate([imag_top, imag[TILE:h]], axis=0).astype(jnp.bfloat16)
        crosses.append(jnp.concatenate([real, imag], axis=1))
    back = jnp.dot(
        jnp.concatenate(crosses, axis=0), inverse, preferred_element_type=jnp.float32
    ).astype(jnp.bfloat16)
    place = lax.broadcasted_iota(jnp.int32, (TILE, 1), 0).astype(jnp.float32) + float(h)
    for c in range(0, cols, 2):
        sides = []
        for d in (c, c + 1):
            mine = back[d * h : (d + 1) * h]
            sides.append(jnp.concatenate([mine[:, :n], mine[:, n:]], axis=0))
        corr = jnp.dot(last, jnp.concatenate(sides, axis=1), preferred_element_type=jnp.float32)
        power = corr * corr
        total = power[:TILE]
        ramp = total
        for t in range(1, n // TILE):
            total = total + power[t * TILE : (t + 1) * TILE]
            ramp = ramp + total
        shifted = place * total - float(TILE) * ramp
        total = jnp.sum(total, axis=0, keepdims=True)
        shifted = jnp.sum(shifted, axis=0, keepdims=True)
        for d in (0, 1):
            put(c + d, shifted[:, d * n : (d + 1) * n], total[:, d * n : (d + 1) * n])


def left_share(boundary, groups, units):
    return units * (groups - 1 - boundary) // groups


def late_cells(groups, local, reach, heap, window):
    units = reach * heap
    halves = 2 * units
    cells = []
    for g in range(groups):
        near = left_share(g, groups, halves) if g < groups - 1 else 0
        before = left_share(g - 1, groups, halves) if g else halves
        right = [("right", k) for k in range((near + 1) // 2)]
        left = [("left", k) for k in range((halves - before + 1) // 2)]
        order = (right + left) if g % 2 else (left + right)
        mine = {}
        for side, k in order[-window:]:
            if side == "right":
                b, h = k // heap, k % heap
                items = [(a, b) for a in range(reach - b)]
            else:
                a, h = k // heap, heap - 1 - k % heap
                items = [(a, b) for b in range((before // 2 + heap - 1 - h) // heap, reach - a)]
            for a, b in items:
                section = (g if side == "right" else g - 1) * local + local - 1 - a
                for part in (0, 1):
                    cut = near if side == "right" else before
                    if cut % 2 and b * heap + h == cut // 2 and part == (side == "right"):
                        continue
                    key = (a + b, 2 * h + part)
                    if key in mine:
                        return None
                    mine[key] = section
        cells.append(mine)
    return cells


def kernel(
    sizes, patches, tab_in, nodes_in, flags_in, field, weight,
    tab, x, nodes, flags, from_right, from_left, spec, halo, stats, slots, combs, late, lates,
    tab_sem, small_sem, own_sem, left_send, left_recv, right_send, right_recv, send, recv, chain,
    group_send, group_recv, tile_send, tile_recv,
):
    groups, tiles, local, reach, rows, cols, n, width, window, cells = sizes
    half = LANES // 2
    part = n // 2 + TILE
    span = rows * cols
    parts = cols // width
    heap = rows * parts
    units = reach * heap
    sec = lax.axis_index("sec")
    tile = lax.axis_index("tile")

    lates[...] = jnp.zeros_like(lates)
    barrier = pltpu.get_barrier_semaphore()

    for d in range(1, tiles):
        pl.semaphore_signal(
            barrier, inc=1, device_id=(sec, (tile + d) % tiles), device_id_type=MESH
        )

    @pl.when(sec > 0)
    def _():
        pl.semaphore_signal(barrier, inc=1, device_id=(sec - 1, tile), device_id_type=MESH)

    @pl.when(sec < groups - 1)
    def _():
        pl.semaphore_signal(barrier, inc=1, device_id=(sec + 1, tile), device_id_type=MESH)

    tab_copy = pltpu.make_async_copy(tab_in, tab, tab_sem)
    tab_copy.start()

    def own_copy(s):
        return pltpu.make_async_copy(patches.at[s], x.at[s], own_sem.at[s])

    for s in range(local):
        own_copy(s).start()
    node_copy = pltpu.make_async_copy(nodes_in, nodes, small_sem.at[0])
    flag_copy = pltpu.make_async_copy(flags_in, flags, small_sem.at[1])
    node_copy.start()
    flag_copy.start()

    halves = 2 * units
    has_left = (sec + groups - 1) // groups
    has_right = 1 - (sec + 1) // groups
    near = left_share(sec, groups, halves)
    before = left_share(sec - 1, groups, halves)
    sent_left = has_left * ((before + 1) // 2)
    sent_right = has_right * ((halves - near + 1) // 2)
    got_right = has_right * ((near + 1) // 2)
    got_left = has_left * ((halves - before + 1) // 2)
    odd_near, odd_before = near % 2, before % 2

    def spot(h):
        return h // parts, (h % parts) * width

    def copy_left(k, size):
        row, col = spot(k % heap)
        return pltpu.make_async_remote_copy(
            src_ref=patches.at[k // heap, row, pl.ds(col, size)],
            dst_ref=from_right.at[k, pl.ds(0, size)],
            send_sem=left_send.at[k],
            recv_sem=left_recv.at[k],
            device_id=(sec - 1, tile),
            device_id_type=MESH,
        )

    def copy_right(k, size):
        row, col = spot(heap - 1 - k % heap)
        rest = width - size
        return pltpu.make_async_remote_copy(
            src_ref=patches.at[local - 1 - k // heap, row, pl.ds(col + rest, size)],
            dst_ref=from_left.at[k, pl.ds(rest, size)],
            send_sem=right_send.at[k],
            recv_sem=right_recv.at[k],
            device_id=(sec + 1, tile),
            device_id_type=MESH,
        )

    def each(copy, act, k, count, odd, also=True):
        part_unit = (odd == 1) & (k == count - 1) & also

        @pl.when((k >= 0) & (k < count - odd) & also)
        def _():
            act(copy(k, width))

        @pl.when(part_unit)
        def _():
            act(copy(k, width // 2))

    stats[...] = jnp.zeros_like(stats)
    pl.semaphore_wait(barrier, tiles - 1 + has_left + has_right)

    begin = lambda copy: copy.start()
    odd_sec = sec % 2
    hold_left = 1 * odd_sec
    hold_right = 1 - hold_left

    def launch(k, carry):
        each(copy_left, begin, k, sent_left, odd_before, k < sent_left - hold_left)
        each(copy_right, begin, k, sent_right, odd_near, k < sent_right - hold_right)
        return carry

    def launch_held(k, carry):
        each(copy_left, begin, k, sent_left, odd_before, k >= sent_left - hold_left)
        each(copy_right, begin, k, sent_right, odd_near, k >= sent_right - hold_right)
        return carry

    def tell():
        @pl.when(sec > 0)
        def _():
            pl.semaphore_signal(chain.at[1], inc=1, device_id=(sec - 1, tile), device_id_type=MESH)

        @pl.when(sec < groups - 1)
        def _():
            pl.semaphore_signal(chain.at[0], inc=1, device_id=(sec + 1, tile), device_id_type=MESH)

    rounds = groups - 2

    def relay(s, carry):
        @pl.when((s < rounds) & (sec > 0))
        def _():
            pl.semaphore_wait(chain.at[0], 1)

        @pl.when((s < rounds) & (sec < groups - 1))
        def _():
            pl.semaphore_wait(chain.at[1], 1)

        @pl.when(s + 1 < rounds)
        def _():
            tell()

        return carry

    lax.fori_loop(0, units, launch, 0)
    if rounds > 0:
        tell()

    tab_copy.wait()
    forward, inverse = open_tables(tab, n)

    def keep(index, offset, base, low=None, high=None, fresh=False):
        index = jnp.where(fresh, local + reach, index)

        def put(c, shifted, total):
            valid = low if c < width // 2 else high
            if valid is not None:
                shifted = jnp.where(valid, shifted, 0.0)
                total = jnp.where(valid, total, 0.0)
            at = (offset - 1) * span + base + c
            stats[index, pl.ds(at, 1), :] = shifted
            stats[index, pl.ds(half + at, 1), :] = total

        return put

    def own(s, carry):
        own_copy(s).wait()
        for row in range(rows):

            def put(c, real, imag):
                spec[s, row, c, :part] = real
                spec[s, row, c, part:] = imag

            spectra(x.at[s, row], *forward, put)

        def body(offset, carry):
            for row in range(rows):
                pairs(
                    lambda c: spec[s - offset, row, c],
                    lambda c: spec[s, row, c],
                    cols, n, *inverse, keep(s - offset, offset, row * cols),
                )
            return carry

        lax.fori_loop(1, jnp.minimum(s, reach) + 1, body, 0)
        return relay(s, carry)

    lax.fori_loop(0, local, own, 0)
    lax.fori_loop(local, rounds, relay, 0)

    area = float(n * n)
    mine = tile * groups + sec

    def ratios(index):
        sub = lax.broadcasted_iota(jnp.int32, (TILE, n), 0)
        lane = lax.broadcasted_iota(jnp.int32, (TILE, n), 1)
        shift = jnp.where(lane < n // 2, lane, lane - n).astype(jnp.float32)
        weigh = jnp.where(sub == 0, 1.0, jnp.where(sub == 1, shift, 0.0))
        red = lax.dot_general(
            weigh,
            stats[index],
            (((1,), (1,)), ((), ())),
            precision=lax.Precision.HIGHEST,
            preferred_element_type=jnp.float32,
        )
        above, along = red[0:1], red[1:2]
        low = lax.broadcasted_iota(jnp.int32, (1, LANES), 1) < half
        total = jnp.where(low, pltpu.roll(above, half, 1), above) / area + EPSILON
        return jnp.where(low, above, along) / area / total

    def group_copy(source, other):
        return pltpu.make_async_remote_copy(
            src_ref=slots.at[source],
            dst_ref=slots.at[source],
            send_sem=group_send.at[other],
            recv_sem=group_recv.at[source],
            device_id=(other, tile),
            device_id_type=MESH,
        )

    def tile_copy(column, other):
        return pltpu.make_async_remote_copy(
            src_ref=combs.at[column],
            dst_ref=combs.at[column],
            send_sem=tile_send.at[other],
            recv_sem=tile_recv.at[column],
            device_id=(sec, other),
            device_id_type=MESH,
        )

    def groups_else(act):
        def visit(d, carry):
            act((sec + d) % groups)
            return carry

        lax.fori_loop(1, groups, visit, 0)

    def columns(act):
        def visit(d, carry):
            act((tile + d) % tiles)
            return carry

        lax.fori_loop(1, tiles, visit, 0)

    def publish():
        node_copy.wait()
        flag_copy.wait()
        slots[sec] = jnp.zeros(slots.shape[1:], jnp.float32)
        for index in range(local + reach):
            at = index if index < local else 2 * local + reach - index
            slots[sec, at : at + 1] = ratios(index)
        for comp in range(2):
            for row in range(rows):
                at = comp * half + reach * span + row * cols
                slots[sec, :local, at : at + cols] = nodes[comp, :, row, :]
        for v in range(reach):
            slots[sec, local : local + 1, v * local : (v + 1) * local] = flags[v : v + 1, :].astype(
                jnp.float32
            )
        groups_else(lambda other: group_copy(sec, other).start())
        lax.fori_loop(0, units, launch_held, 0)

    def spread_columns():
        groups_else(lambda other: group_copy(other, other).wait_recv())
        groups_else(lambda other: group_copy(sec, other).wait_send())
        for g in range(groups):
            block = slots[g, :local]
            if g < groups - 1:
                add = slots[g + 1, local + 1 :]
                block = jnp.concatenate([block[: local - reach], block[local - reach :] + add], axis=0)
            combs[tile, g * local : (g + 1) * local] = block
        columns(lambda other: tile_copy(tile, other).start())


    def put_halo(c, real, imag):
        halo[c, :part] = real
        halo[c, part:] = imag

    got = got_right + got_left

    def far(k, carry):
        fresh = k >= got - window
        pl.when(k == got - window)(publish)
        if window > 1:
            pl.when(k == got - 1)(spread_columns)

        u = k - odd_sec * got_right
        k = k - (1 - odd_sec) * got_left

        done = lambda copy: copy.wait_recv()
        each(copy_left, done, k, got_right, odd_near)
        each(copy_right, done, u, got_left, odd_before)
        from_next = (k >= 0) & (k < got_right)
        from_last = (u >= 0) & (u < got_left)
        next_spot = k % heap
        last_spot = heap - 1 - u % heap
        first = (before // 2 + heap - 1 - last_spot) // heap

        for many in range(1, reach + 1):

            @pl.when(from_next & (reach - k // heap == many))
            def _():
                spectra(from_right.at[k], *forward, put_halo)
                row, col = spot(next_spot)
                whole = (odd_near == 0) | (k < got_right - 1)
                for a in range(many):
                    pairs(
                        lambda c: spec[local - 1 - a, row, col + c],
                        lambda c: halo[c],
                        width, n, *inverse,
                        keep(local - 1 - a, a + reach - many + 1, next_spot * width, None, whole, fresh),
                    )

            @pl.when(from_last & (reach - u // heap - first == many))
            def _():
                spectra(from_left.at[u], *forward, put_halo)
                row, col = spot(last_spot)
                a = u // heap
                for d in range(many):
                    b = first + d
                    whole = (odd_before == 0) | (b * heap + last_spot > before // 2)
                    pairs(
                        lambda c: halo[c],
                        lambda c: spec[b, row, col + c],
                        width, n, *inverse,
                        keep(local + a, a + b + 1, last_spot * width, whole, None, fresh),
                    )

        return carry

    lax.fori_loop(0, got, far, 0)

    if window == 1:
        spread_columns()
    late[...] = ratios(local + reach)

    far_off = min(groups - 1, -(-SWEEPS * reach // local))
    deltas = sorted(range(-far_off, far_off + 1), key=lambda delta: -abs(delta))

    def late_copy(delta, to):
        return pltpu.make_async_remote_copy(
            src_ref=late,
            dst_ref=lates.at[mine],
            send_sem=send.at[delta + far_off],
            recv_sem=recv.at[delta + far_off],
            device_id=(sec + delta, to),
            device_id_type=MESH,
        )

    def late_sum(delta):
        several = lates.at[pl.ds(0, tiles if delta else tiles - 1)]
        return pltpu.make_async_remote_copy(
            src_ref=several,
            dst_ref=several,
            send_sem=send.at[delta + far_off],
            recv_sem=recv.at[delta + far_off],
            device_id=(sec, (tile + 1) % tiles),
            device_id_type=MESH,
        )

    def peers(sign, act):
        for delta in deltas:
            to = sec + sign * delta
            pl.when((to >= 0) & (to < groups))(functools.partial(act, delta))

    def send_late(delta):
        for d in range(0 if delta else 1, tiles):
            late_copy(delta, (tile + d) % tiles).start()

    peers(1, send_late)
    lates[mine] = late[...]

    def sent(k, carry):
        done = lambda copy: copy.wait_send()
        each(copy_left, done, k, sent_left, odd_before)
        each(copy_right, done, k, sent_right, odd_near)
        return carry

    lax.fori_loop(0, units, sent, 0)

    lane = lax.broadcasted_iota(jnp.int32, (TILE, LANES), 1)
    sub = lax.broadcasted_iota(jnp.int32, (TILE, LANES), 0)
    total = groups * local
    for g in range(groups):
        flat = jnp.broadcast_to(slots[g, local : local + 1], (TILE, LANES))
        for v in range(reach):
            w = jnp.sum(jnp.where(lane == v * local + sub, flat, 0.0), axis=1, keepdims=True)
            w = jnp.broadcast_to(w, (TILE, LANES))
            w = jnp.where(g * local + sub + v + 1 < total, w, 0.0)
            weight[v, g * local : (g + 1) * local, :] = w[:local]
    columns(lambda other: tile_copy(other, other).wait_recv())
    owner = lax.broadcasted_iota(jnp.int32, (total, LANES), 1) % half // span
    for v in range(reach + 1):
        value = jnp.zeros((total, LANES), jnp.float32)
        for t in range(tiles):
            block = combs[t]
            if t != v:
                block = pltpu.roll(block, (t - v) * span % LANES, 1)
            value = jnp.where(owner == t, block, value)
        field[v] = value * weight[v] if v < reach else value

    peers(-1, lambda delta: late_sum(delta).wait_recv())
    slot = lax.broadcasted_iota(jnp.int32, (1, LANES), 1) % span // (width // 2)
    column = lax.broadcasted_iota(jnp.int32, (groups, LANES), 1) % half // span
    blocks = [lates[pl.ds(t * groups, groups), 0, :] for t in range(tiles)]
    for v in range(reach):
        value = jnp.zeros((groups, LANES), jnp.float32)
        for t in range(tiles):
            block = blocks[t]
            if t != v:
                block = pltpu.roll(block, (t - v) * span % LANES, 1)
            value = jnp.where(column == t, block, value)
        for g in range(groups):
            found = {}
            for (o, part), section in sorted(cells[g].items()):
                if o == v:
                    found.setdefault(section, []).append(part)
            for section, places in sorted(found.items()):
                line = value[g : g + 1]
                if len(found) > 1:
                    inside = slot == places[0]
                    for part in places[1:]:
                        inside = inside | (slot == part)
                    line = jnp.where(inside, line, 0.0)
                here = slice(section, section + 1)
                field[v, here, :] = field[v, here, :] + line * weight[v, here, :]

    columns(lambda other: tile_copy(tile, other).wait_send())
    peers(1, lambda delta: late_sum(delta).wait_send())


def relax(sizes, field, weight, moved, shown, final):
    groups, tiles, local, reach, rows, cols = sizes[:6]
    half = LANES // 2
    span = rows * cols
    total = groups * local
    sec = lax.axis_index("sec")
    tile = lax.axis_index("tile")
    grid_rows = tiles * rows
    at = lax.broadcasted_iota(jnp.int32, (total, LANES), 1) % half
    across = at % cols
    down = at // cols
    one = lambda mask: mask.astype(jnp.float32)
    left, right = one(across > 0), one(across < cols - 1)
    up, below = one(down > 0), one(down < grid_rows - 1)

    def sweep(_, u):
        plane = (
            up * (pltpu.roll(u, cols, 1) - u)
            + below * (pltpu.roll(u, LANES - cols, 1) - u)
            + left * (pltpu.roll(u, 1, 1) - u)
            + right * (pltpu.roll(u, LANES - 1, 1) - u)
        )
        spring = jnp.zeros_like(u)
        for v in range(reach):
            o = v + 1
            r = weight[v] * (pltpu.roll(u, total - o, 0) - u) - field[v]
            spring = spring + r - pltpu.roll(r, o, 0)
        return u + STEP_SIZE * (plane + spring)

    final[...] = lax.fori_loop(0, SWEEPS, sweep, field[reach])
    back = (LANES - tile * span) % LANES
    for v in range(reach + 1):
        source = field.at[v] if v < reach else final
        mine = pltpu.roll(source[pl.ds(sec * local, local), :], back, 1)
        for comp in range(2):
            for row in range(rows):
                at = comp * half + row * cols
                piece = mine[:, at : at + cols]
                if v < reach:
                    shown[comp, :, v, row, :] = piece
                else:
                    moved[comp, :, row, :] = piece


def shards(patches, pair_flags, nodes):
    local, rows, cols, n = patches.shape[:4]
    reach = pair_flags.shape[1]
    groups, tiles = lax.axis_size("sec"), lax.axis_size("tile")
    part = n // 2 + TILE
    width = cols // 2
    units = reach * rows * cols // width
    tab = jnp.asarray(tables(n))
    heap = units // reach
    window = 3
    while window > 1 and late_cells(groups, local, reach, heap, window) is None:
        window -= 1
    cells = late_cells(groups, local, reach, heap, window)
    sizes = (groups, tiles, local, reach, rows, cols, n, width, window, cells)
    hbm = pl.BlockSpec(memory_space=pltpu.HBM)
    vmem = pl.BlockSpec(memory_space=pltpu.VMEM)
    dma = pltpu.SemaphoreType.DMA
    field, weight = pl.pallas_call(
        functools.partial(kernel, sizes),
        in_specs=[hbm] * 4,
        out_specs=[vmem] * 2,
        out_shape=[
            jax.ShapeDtypeStruct((reach + 1, groups * local, LANES), jnp.float32),
            jax.ShapeDtypeStruct((reach, groups * local, LANES), jnp.float32),
        ],
        scratch_shapes=[
            pltpu.VMEM(tab.shape, jnp.bfloat16),
            pltpu.VMEM((local, rows, cols, n, n), jnp.bfloat16),
            pltpu.VMEM(nodes.shape, jnp.float32),
            pltpu.VMEM((reach, local), jnp.int32),
            pltpu.VMEM((units, width, n, n), jnp.bfloat16),
            pltpu.VMEM((units, width, n, n), jnp.bfloat16),
            pltpu.VMEM((local, rows, cols, 2 * part, n), jnp.float32),
            pltpu.VMEM((width, 2 * part, n), jnp.float32),
            pltpu.VMEM((local + reach + 1, LANES, LANES), jnp.float32),
            pltpu.VMEM((groups, local + reach + 1, LANES), jnp.float32),
            pltpu.VMEM((tiles, groups * local, LANES), jnp.float32),
            pltpu.VMEM((1, LANES), jnp.float32),
            pltpu.VMEM((groups * tiles, 1, LANES), jnp.float32),
            dma,
            dma((2,)),
            dma((local,)),
            dma((units,)),
            dma((units,)),
            dma((units,)),
            dma((units,)),
            dma((2 * groups,)),
            dma((2 * groups,)),
            pltpu.SemaphoreType.REGULAR((2,)),
            dma((groups,)),
            dma((groups,)),
            dma((tiles,)),
            dma((tiles,)),
        ],
        compiler_params=pltpu.CompilerParams(
            collective_id=0, has_side_effects=True, vmem_limit_bytes=48 << 20
        ),
        name="align",
    )(*[pltpu.with_memory_space_constraint(a, pltpu.HBM) for a in (patches, tab, nodes, pair_flags.T)])
    return pl.pallas_call(
        functools.partial(relax, sizes),
        in_specs=[vmem] * 2,
        out_specs=[vmem] * 2,
        out_shape=[
            jax.ShapeDtypeStruct((2, local, rows, cols), jnp.float32),
            jax.ShapeDtypeStruct((2, local, reach, rows, cols), jnp.float32),
        ],
        scratch_shapes=[pltpu.VMEM((groups * local, LANES), jnp.float32)],
        compiler_params=pltpu.CompilerParams(vmem_limit_bytes=8 << 20),
        name="relax",
    )(field, weight)


def solution(mesh):
    placed = (P("sec", "tile", None, None, None), P("sec", None), P(None, "sec", "tile", None))
    return jax.shard_map(
        shards,
        mesh=mesh,
        in_specs=placed,
        out_specs=(P(None, "sec", "tile", None), P(None, "sec", None, "tile", None)),
        check_vma=False,
    )
```

```python
import functools
import math

import jax
import jax.numpy as jnp
import numpy as np
from jax import lax
from jax.experimental import pallas as pl
from jax.experimental.pallas import tpu as pltpu
from jax.sharding import PartitionSpec as P

SWEEPS = 8
STEP_SIZE = 0.08
EPSILON = 1e-06
LANES = 128
TILE = 8
MESH = pl.DeviceIdType.MESH


def tables(n):
    h = n // 2
    k = np.arange(n)
    phase = (k[:, None] * k[None, :] % n) * (2.0 * math.pi / n)
    c = np.asarray(np.cos(phase), np.float32).astype(jnp.bfloat16).astype(np.float32)
    s = np.asarray(np.sin(phase), np.float32).astype(jnp.bfloat16).astype(np.float32)
    part = h + TILE
    first = np.zeros((2 * part, 2 * n), np.float32)
    first[: h + 1, :n] = c[: h + 1]
    first[part : part + h, :n] = s[:h]
    second = np.concatenate([np.concatenate([c, -s], 1), np.concatenate([-s, -c], 1)], 0)
    inverse = np.concatenate([np.concatenate([c, s], 1), np.concatenate([-s, c], 1)], 0)
    order = (np.arange(n) - h) % n
    last = np.zeros((n, 2 * n), np.float32)
    last[:, 0] = c[order, 0]
    last[:, 1:h] = 2.0 * c[order, 1:h]
    last[:, h] = c[order, h]
    last[:, h + 1 : n] = -2.0 * s[order, 1:h]
    last *= 1.0 / float(n) ** 3
    return np.concatenate([first, second, inverse, last], 0).astype(jnp.bfloat16)


def open_tables(tab, n):
    part = n // 2 + TILE
    first = tab[: 2 * part, :n]
    second = tab[2 * part : 2 * part + 2 * n]
    inverse = tab[2 * part + 2 * n : 2 * part + 4 * n]
    last = tab[2 * part + 4 * n :, :n]
    return (first, second), (inverse, last)


def spectra(x, first, second, put):
    cols, n = x.shape[0], x.shape[-1]
    part = n // 2 + TILE
    lines = []
    for c in range(0, cols, 2):
        y = jnp.dot(
            first, jnp.concatenate([x[c], x[c + 1]], axis=1), preferred_element_type=jnp.float32
        )
        for d in (0, 1):
            mine = y[:, d * n : (d + 1) * n]
            lines.append(jnp.concatenate([mine[:part], mine[part:]], axis=1))
    lines = jnp.concatenate(lines, axis=0).astype(jnp.bfloat16)
    spec = jnp.dot(lines, second, preferred_element_type=jnp.float32)
    for c in range(cols):
        mine = spec[c * part : (c + 1) * part]
        put(c, mine[:, :n], mine[:, n:])


def pairs(get_a, get_b, cols, n, inverse, last, put):
    h = n // 2
    part = h + TILE
    crosses = []
    for c in range(cols):
        a, b = get_a(c), get_b(c)
        ar, ai, br, bi = a[:part], a[part:], b[:part], b[part:]
        real = ar * br + ai * bi
        imag = ar * bi - ai * br
        real_top = real[:TILE] - imag[h:]
        imag_top = imag[:TILE] + real[h:]
        real = jnp.concatenate([real_top, real[TILE:h]], axis=0).astype(jnp.bfloat16)
        imag = jnp.concatenate([imag_top, imag[TILE:h]], axis=0).astype(jnp.bfloat16)
        crosses.append(jnp.concatenate([real, imag], axis=1))
    back = jnp.dot(
        jnp.concatenate(crosses, axis=0), inverse, preferred_element_type=jnp.float32
    ).astype(jnp.bfloat16)
    place = lax.broadcasted_iota(jnp.int32, (TILE, 1), 0).astype(jnp.float32) + float(h)
    for c in range(0, cols, 2):
        sides = []
        for d in (c, c + 1):
            mine = back[d * h : (d + 1) * h]
            sides.append(jnp.concatenate([mine[:, :n], mine[:, n:]], axis=0))
        corr = jnp.dot(last, jnp.concatenate(sides, axis=1), preferred_element_type=jnp.float32)
        power = corr * corr
        total = power[:TILE]
        ramp = total
        for t in range(1, n // TILE):
            total = total + power[t * TILE : (t + 1) * TILE]
            ramp = ramp + total
        shifted = place * total - float(TILE) * ramp
        total = jnp.sum(total, axis=0, keepdims=True)
        shifted = jnp.sum(shifted, axis=0, keepdims=True)
        for d in (0, 1):
            put(c + d, shifted[:, d * n : (d + 1) * n], total[:, d * n : (d + 1) * n])


def left_share(boundary, groups, units):
    return units * (groups - 1 - boundary) // groups


def late_cells(groups, local, reach, heap, window):
    units = reach * heap
    halves = 2 * units
    cells = []
    for g in range(groups):
        near = left_share(g, groups, halves) if g < groups - 1 else 0
        before = left_share(g - 1, groups, halves) if g else halves
        right = [("right", k) for k in range((near + 1) // 2)]
        left = [("left", k) for k in range((halves - before + 1) // 2)]
        order = (right + left) if g % 2 else (left + right)
        mine = {}
        for side, k in order[-window:]:
            if side == "right":
                b, h = k // heap, k % heap
                items = [(a, b) for a in range(reach - b)]
            else:
                a, h = k // heap, heap - 1 - k % heap
                items = [(a, b) for b in range((before // 2 + heap - 1 - h) // heap, reach - a)]
            for a, b in items:
                section = (g if side == "right" else g - 1) * local + local - 1 - a
                for part in (0, 1):
                    cut = near if side == "right" else before
                    if cut % 2 and b * heap + h == cut // 2 and part == (side == "right"):
                        continue
                    key = (a + b, 2 * h + part)
                    if key in mine:
                        return None
                    mine[key] = section
        cells.append(mine)
    return cells


def kernel(
    sizes, patches, tab_in, nodes_in, flags_in, field, weight,
    tab, x, nodes, flags, from_right, from_left, spec, halo, stats, slots, combs, late, lates,
    tab_sem, small_sem, own_sem, left_send, left_recv, right_send, right_recv, send, recv, chain,
    group_send, group_recv, tile_send, tile_recv,
):
    groups, tiles, local, reach, rows, cols, n, width, window, cells = sizes
    half = LANES // 2
    part = n // 2 + TILE
    span = rows * cols
    parts = cols // width
    heap = rows * parts
    units = reach * heap
    sec = lax.axis_index("sec")
    tile = lax.axis_index("tile")

    lates[...] = jnp.zeros_like(lates)
    barrier = pltpu.get_barrier_semaphore()

    for d in range(1, tiles):
        pl.semaphore_signal(
            barrier, inc=1, device_id=(sec, (tile + d) % tiles), device_id_type=MESH
        )

    @pl.when(sec > 0)
    def _():
        pl.semaphore_signal(barrier, inc=1, device_id=(sec - 1, tile), device_id_type=MESH)

    @pl.when(sec < groups - 1)
    def _():
        pl.semaphore_signal(barrier, inc=1, device_id=(sec + 1, tile), device_id_type=MESH)

    tab_copy = pltpu.make_async_copy(tab_in, tab, tab_sem)
    tab_copy.start()

    def own_copy(s):
        return pltpu.make_async_copy(patches.at[s], x.at[s], own_sem.at[s])

    for s in range(local):
        own_copy(s).start()
    node_copy = pltpu.make_async_copy(nodes_in, nodes, small_sem.at[0])
    flag_copy = pltpu.make_async_copy(flags_in, flags, small_sem.at[1])
    node_copy.start()
    flag_copy.start()

    halves = 2 * units
    has_left = (sec + groups - 1) // groups
    has_right = 1 - (sec + 1) // groups
    near = left_share(sec, groups, halves)
    before = left_share(sec - 1, groups, halves)
    sent_left = has_left * ((before + 1) // 2)
    sent_right = has_right * ((halves - near + 1) // 2)
    got_right = has_right * ((near + 1) // 2)
    got_left = has_left * ((halves - before + 1) // 2)
    odd_near, odd_before = near % 2, before % 2

    def spot(h):
        return h // parts, (h % parts) * width

    def copy_left(k, size):
        row, col = spot(k % heap)
        return pltpu.make_async_remote_copy(
            src_ref=patches.at[k // heap, row, pl.ds(col, size)],
            dst_ref=from_right.at[k, pl.ds(0, size)],
            send_sem=left_send.at[k],
            recv_sem=left_recv.at[k],
            device_id=(sec - 1, tile),
            device_id_type=MESH,
        )

    def copy_right(k, size):
        row, col = spot(heap - 1 - k % heap)
        rest = width - size
        return pltpu.make_async_remote_copy(
            src_ref=patches.at[local - 1 - k // heap, row, pl.ds(col + rest, size)],
            dst_ref=from_left.at[k, pl.ds(rest, size)],
            send_sem=right_send.at[k],
            recv_sem=right_recv.at[k],
            device_id=(sec + 1, tile),
            device_id_type=MESH,
        )

    def each(copy, act, k, count, odd, also=True):
        part_unit = (odd == 1) & (k == count - 1) & also

        @pl.when((k >= 0) & (k < count - odd) & also)
        def _():
            act(copy(k, width))

        @pl.when(part_unit)
        def _():
            act(copy(k, width // 2))

    stats[...] = jnp.zeros_like(stats)
    pl.semaphore_wait(barrier, tiles - 1 + has_left + has_right)

    begin = lambda copy: copy.start()
    odd_sec = sec % 2
    hold_left = 1 * odd_sec
    hold_right = 1 - hold_left

    def launch(k, carry):
        each(copy_left, begin, k, sent_left, odd_before, k < sent_left - hold_left)
        each(copy_right, begin, k, sent_right, odd_near, k < sent_right - hold_right)
        return carry

    def launch_held(k, carry):
        each(copy_left, begin, k, sent_left, odd_before, k >= sent_left - hold_left)
        each(copy_right, begin, k, sent_right, odd_near, k >= sent_right - hold_right)
        return carry

    def tell():
        @pl.when(sec > 0)
        def _():
            pl.semaphore_signal(chain.at[1], inc=1, device_id=(sec - 1, tile), device_id_type=MESH)

        @pl.when(sec < groups - 1)
        def _():
            pl.semaphore_signal(chain.at[0], inc=1, device_id=(sec + 1, tile), device_id_type=MESH)

    rounds = groups - 2

    def relay(s, carry):
        @pl.when((s < rounds) & (sec > 0))
        def _():
            pl.semaphore_wait(chain.at[0], 1)

        @pl.when((s < rounds) & (sec < groups - 1))
        def _():
            pl.semaphore_wait(chain.at[1], 1)

        @pl.when(s + 1 < rounds)
        def _():
            tell()

        return carry

    lax.fori_loop(0, units, launch, 0)
    if rounds > 0:
        tell()

    tab_copy.wait()
    forward, inverse = open_tables(tab, n)

    def keep(index, offset, base, low=None, high=None, fresh=False):
        index = jnp.where(fresh, local + reach, index)

        def put(c, shifted, total):
            valid = low if c < width // 2 else high
            if valid is not None:
                shifted = jnp.where(valid, shifted, 0.0)
                total = jnp.where(valid, total, 0.0)
            at = (offset - 1) * span + base + c
            stats[index, pl.ds(at, 1), :] = shifted
            stats[index, pl.ds(half + at, 1), :] = total

        return put

    def own(s, carry):
        own_copy(s).wait()
        for row in range(rows):

            def put(c, real, imag):
                spec[s, row, c, :part] = real
                spec[s, row, c, part:] = imag

            spectra(x.at[s, row], *forward, put)

        def body(offset, carry):
            for row in range(rows):
                pairs(
                    lambda c: spec[s - offset, row, c],
                    lambda c: spec[s, row, c],
                    cols, n, *inverse, keep(s - offset, offset, row * cols),
                )
            return carry

        lax.fori_loop(1, jnp.minimum(s, reach) + 1, body, 0)
        return relay(s, carry)

    lax.fori_loop(0, local, own, 0)
    lax.fori_loop(local, rounds, relay, 0)

    area = float(n * n)
    mine = tile * groups + sec

    def ratios(index):
        sub = lax.broadcasted_iota(jnp.int32, (TILE, n), 0)
        lane = lax.broadcasted_iota(jnp.int32, (TILE, n), 1)
        shift = jnp.where(lane < n // 2, lane, lane - n).astype(jnp.float32)
        weigh = jnp.where(sub == 0, 1.0, jnp.where(sub == 1, shift, 0.0))
        red = lax.dot_general(
            weigh,
            stats[index],
            (((1,), (1,)), ((), ())),
            precision=lax.Precision.HIGHEST,
            preferred_element_type=jnp.float32,
        )
        above, along = red[0:1], red[1:2]
        low = lax.broadcasted_iota(jnp.int32, (1, LANES), 1) < half
        total = jnp.where(low, pltpu.roll(above, half, 1), above) / area + EPSILON
        return jnp.where(low, above, along) / area / total

    def group_copy(source, other):
        return pltpu.make_async_remote_copy(
            src_ref=slots.at[source],
            dst_ref=slots.at[source],
            send_sem=group_send.at[other],
            recv_sem=group_recv.at[source],
            device_id=(other, tile),
            device_id_type=MESH,
        )

    def tile_copy(column, other):
        return pltpu.make_async_remote_copy(
            src_ref=combs.at[column],
            dst_ref=combs.at[column],
            send_sem=tile_send.at[other],
            recv_sem=tile_recv.at[column],
            device_id=(sec, other),
            device_id_type=MESH,
        )

    def groups_else(act):
        def visit(d, carry):
            act((sec + d) % groups)
            return carry

        lax.fori_loop(1, groups, visit, 0)

    def columns(act):
        def visit(d, carry):
            act((tile + d) % tiles)
            return carry

        lax.fori_loop(1, tiles, visit, 0)

    def publish():
        node_copy.wait()
        flag_copy.wait()
        slots[sec] = jnp.zeros(slots.shape[1:], jnp.float32)
        for index in range(local + reach):
            at = index if index < local else 2 * local + reach - index
            slots[sec, at : at + 1] = ratios(index)
        for comp in range(2):
            for row in range(rows):
                at = comp * half + reach * span + row * cols
                slots[sec, :local, at : at + cols] = nodes[comp, :, row, :]
        for v in range(reach):
            slots[sec, local : local + 1, v * local : (v + 1) * local] = flags[v : v + 1, :].astype(
                jnp.float32
            )
        groups_else(lambda other: group_copy(sec, other).start())
        lax.fori_loop(0, units, launch_held, 0)

    def spread_columns():
        groups_else(lambda other: group_copy(other, other).wait_recv())
        groups_else(lambda other: group_copy(sec, other).wait_send())
        for g in range(groups):
            block = slots[g, :local]
            if g < groups - 1:
                add = slots[g + 1, local + 1 :]
                block = jnp.concatenate([block[: local - reach], block[local - reach :] + add], axis=0)
            combs[tile, g * local : (g + 1) * local] = block
        columns(lambda other: tile_copy(tile, other).start())


    def put_halo(c, real, imag):
        halo[c, :part] = real
        halo[c, part:] = imag

    got = got_right + got_left

    def far(k, carry):
        fresh = k >= got - window
        pl.when(k == got - window)(publish)
        if window > 1:
            pl.when(k == got - 1)(spread_columns)

        u = k - odd_sec * got_right
        k = k - (1 - odd_sec) * got_left

        done = lambda copy: copy.wait_recv()
        each(copy_left, done, k, got_right, odd_near)
        each(copy_right, done, u, got_left, odd_before)
        from_next = (k >= 0) & (k < got_right)
        from_last = (u >= 0) & (u < got_left)
        next_spot = k % heap
        last_spot = heap - 1 - u % heap
        first = (before // 2 + heap - 1 - last_spot) // heap

        end_next = (odd_near == 1) & (k == got_right - 1)
        end_last = (odd_before == 1) & (u == got_left - 1)

        def next_unit(many, size):
            spectra(from_right.at[k, pl.ds(0, size)], *forward, put_halo)
            row, col = spot(next_spot)
            for a in range(many):
                pairs(
                    lambda c: spec[local - 1 - a, row, col + c],
                    lambda c: halo[c],
                    size, n, *inverse,
                    keep(local - 1 - a, a + reach - many + 1, next_spot * width, fresh=fresh),
                )

        def last_unit(many, size):
            rest = width - size
            spectra(from_left.at[u, pl.ds(rest, size)], *forward, put_halo)
            row, col = spot(last_spot)
            a = u // heap
            for d in range(many):
                b = first + d
                whole = None
                if size == width:
                    whole = (odd_before == 0) | (b * heap + last_spot > before // 2)
                pairs(
                    lambda c: halo[c],
                    lambda c: spec[b, row, col + rest + c],
                    size, n, *inverse,
                    keep(local + a, a + b + 1, last_spot * width + rest, whole, None, fresh),
                )

        for many in range(1, reach + 1):
            next_many = from_next & (reach - k // heap == many)
            last_many = from_last & (reach - u // heap - first == many)
            pl.when(next_many & jnp.logical_not(end_next))(functools.partial(next_unit, many, width))
            pl.when(next_many & end_next)(functools.partial(next_unit, many, width // 2))
            pl.when(last_many & jnp.logical_not(end_last))(functools.partial(last_unit, many, width))
            pl.when(last_many & end_last)(functools.partial(last_unit, many, width // 2))

        return carry

    lax.fori_loop(0, got, far, 0)

    if window == 1:
        spread_columns()
    late[...] = ratios(local + reach)

    far_off = min(groups - 1, -(-SWEEPS * reach // local))
    deltas = sorted(range(-far_off, far_off + 1), key=lambda delta: -abs(delta))

    def late_copy(delta, to):
        return pltpu.make_async_remote_copy(
            src_ref=late,
            dst_ref=lates.at[mine],
            send_sem=send.at[delta + far_off],
            recv_sem=recv.at[delta + far_off],
            device_id=(sec + delta, to),
            device_id_type=MESH,
        )

    def late_sum(delta):
        several = lates.at[pl.ds(0, tiles if delta else tiles - 1)]
        return pltpu.make_async_remote_copy(
            src_ref=several,
            dst_ref=several,
            send_sem=send.at[delta + far_off],
            recv_sem=recv.at[delta + far_off],
            device_id=(sec, (tile + 1) % tiles),
            device_id_type=MESH,
        )

    def peers(sign, act):
        for delta in deltas:
            to = sec + sign * delta
            pl.when((to >= 0) & (to < groups))(functools.partial(act, delta))

    def send_late(delta):
        for d in range(0 if delta else 1, tiles):
            late_copy(delta, (tile + d) % tiles).start()

    peers(1, send_late)
    lates[mine] = late[...]

    def sent(k, carry):
        done = lambda copy: copy.wait_send()
        each(copy_left, done, k, sent_left, odd_before)
        each(copy_right, done, k, sent_right, odd_near)
        return carry

    lax.fori_loop(0, units, sent, 0)

    lane = lax.broadcasted_iota(jnp.int32, (TILE, LANES), 1)
    sub = lax.broadcasted_iota(jnp.int32, (TILE, LANES), 0)
    total = groups * local
    for g in range(groups):
        flat = jnp.broadcast_to(slots[g, local : local + 1], (TILE, LANES))
        for v in range(reach):
            w = jnp.sum(jnp.where(lane == v * local + sub, flat, 0.0), axis=1, keepdims=True)
            w = jnp.broadcast_to(w, (TILE, LANES))
            w = jnp.where(g * local + sub + v + 1 < total, w, 0.0)
            weight[v, g * local : (g + 1) * local, :] = w[:local]
    columns(lambda other: tile_copy(other, other).wait_recv())
    owner = lax.broadcasted_iota(jnp.int32, (total, LANES), 1) % half // span
    for v in range(reach + 1):
        value = jnp.zeros((total, LANES), jnp.float32)
        for t in range(tiles):
            block = combs[t]
            if t != v:
                block = pltpu.roll(block, (t - v) * span % LANES, 1)
            value = jnp.where(owner == t, block, value)
        field[v] = value * weight[v] if v < reach else value

    peers(-1, lambda delta: late_sum(delta).wait_recv())
    slot = lax.broadcasted_iota(jnp.int32, (1, LANES), 1) % span // (width // 2)
    column = lax.broadcasted_iota(jnp.int32, (groups, LANES), 1) % half // span
    blocks = [lates[pl.ds(t * groups, groups), 0, :] for t in range(tiles)]
    for v in range(reach):
        value = jnp.zeros((groups, LANES), jnp.float32)
        for t in range(tiles):
            block = blocks[t]
            if t != v:
                block = pltpu.roll(block, (t - v) * span % LANES, 1)
            value = jnp.where(column == t, block, value)
        for g in range(groups):
            found = {}
            for (o, part), section in sorted(cells[g].items()):
                if o == v:
                    found.setdefault(section, []).append(part)
            for section, places in sorted(found.items()):
                line = value[g : g + 1]
                if len(found) > 1:
                    inside = slot == places[0]
                    for part in places[1:]:
                        inside = inside | (slot == part)
                    line = jnp.where(inside, line, 0.0)
                here = slice(section, section + 1)
                field[v, here, :] = field[v, here, :] + line * weight[v, here, :]

    columns(lambda other: tile_copy(tile, other).wait_send())
    peers(1, lambda delta: late_sum(delta).wait_send())


def relax(sizes, field, weight, moved, shown, final):
    groups, tiles, local, reach, rows, cols = sizes[:6]
    half = LANES // 2
    span = rows * cols
    total = groups * local
    sec = lax.axis_index("sec")
    tile = lax.axis_index("tile")
    grid_rows = tiles * rows
    at = lax.broadcasted_iota(jnp.int32, (total, LANES), 1) % half
    across = at % cols
    down = at // cols
    one = lambda mask: mask.astype(jnp.float32)
    left, right = one(across > 0), one(across < cols - 1)
    up, below = one(down > 0), one(down < grid_rows - 1)

    def sweep(_, u):
        plane = (
            up * (pltpu.roll(u, cols, 1) - u)
            + below * (pltpu.roll(u, LANES - cols, 1) - u)
            + left * (pltpu.roll(u, 1, 1) - u)
            + right * (pltpu.roll(u, LANES - 1, 1) - u)
        )
        spring = jnp.zeros_like(u)
        for v in range(reach):
            o = v + 1
            r = weight[v] * (pltpu.roll(u, total - o, 0) - u) - field[v]
            spring = spring + r - pltpu.roll(r, o, 0)
        return u + STEP_SIZE * (plane + spring)

    final[...] = lax.fori_loop(0, SWEEPS, sweep, field[reach])
    back = (LANES - tile * span) % LANES
    for v in range(reach + 1):
        source = field.at[v] if v < reach else final
        mine = pltpu.roll(source[pl.ds(sec * local, local), :], back, 1)
        for comp in range(2):
            for row in range(rows):
                at = comp * half + row * cols
                piece = mine[:, at : at + cols]
                if v < reach:
                    shown[comp, :, v, row, :] = piece
                else:
                    moved[comp, :, row, :] = piece


def shards(patches, pair_flags, nodes):
    local, rows, cols, n = patches.shape[:4]
    reach = pair_flags.shape[1]
    groups, tiles = lax.axis_size("sec"), lax.axis_size("tile")
    part = n // 2 + TILE
    width = cols // 2
    units = reach * rows * cols // width
    tab = jnp.asarray(tables(n))
    heap = units // reach
    window = 3
    while window > 1 and late_cells(groups, local, reach, heap, window) is None:
        window -= 1
    cells = late_cells(groups, local, reach, heap, window)
    sizes = (groups, tiles, local, reach, rows, cols, n, width, window, cells)
    hbm = pl.BlockSpec(memory_space=pltpu.HBM)
    vmem = pl.BlockSpec(memory_space=pltpu.VMEM)
    dma = pltpu.SemaphoreType.DMA
    field, weight = pl.pallas_call(
        functools.partial(kernel, sizes),
        in_specs=[hbm] * 4,
        out_specs=[vmem] * 2,
        out_shape=[
            jax.ShapeDtypeStruct((reach + 1, groups * local, LANES), jnp.float32),
            jax.ShapeDtypeStruct((reach, groups * local, LANES), jnp.float32),
        ],
        scratch_shapes=[
            pltpu.VMEM(tab.shape, jnp.bfloat16),
            pltpu.VMEM((local, rows, cols, n, n), jnp.bfloat16),
            pltpu.VMEM(nodes.shape, jnp.float32),
            pltpu.VMEM((reach, local), jnp.int32),
            pltpu.VMEM((units, width, n, n), jnp.bfloat16),
            pltpu.VMEM((units, width, n, n), jnp.bfloat16),
            pltpu.VMEM((local, rows, cols, 2 * part, n), jnp.float32),
            pltpu.VMEM((width, 2 * part, n), jnp.float32),
            pltpu.VMEM((local + reach + 1, LANES, LANES), jnp.float32),
            pltpu.VMEM((groups, local + reach + 1, LANES), jnp.float32),
            pltpu.VMEM((tiles, groups * local, LANES), jnp.float32),
            pltpu.VMEM((1, LANES), jnp.float32),
            pltpu.VMEM((groups * tiles, 1, LANES), jnp.float32),
            dma,
            dma((2,)),
            dma((local,)),
            dma((units,)),
            dma((units,)),
            dma((units,)),
            dma((units,)),
            dma((2 * groups,)),
            dma((2 * groups,)),
            pltpu.SemaphoreType.REGULAR((2,)),
            dma((groups,)),
            dma((groups,)),
            dma((tiles,)),
            dma((tiles,)),
        ],
        compiler_params=pltpu.CompilerParams(
            collective_id=0, has_side_effects=True, vmem_limit_bytes=48 << 20
        ),
        name="align",
    )(*[pltpu.with_memory_space_constraint(a, pltpu.HBM) for a in (patches, tab, nodes, pair_flags.T)])
    return pl.pallas_call(
        functools.partial(relax, sizes),
        in_specs=[vmem] * 2,
        out_specs=[vmem] * 2,
        out_shape=[
            jax.ShapeDtypeStruct((2, local, rows, cols), jnp.float32),
            jax.ShapeDtypeStruct((2, local, reach, rows, cols), jnp.float32),
        ],
        scratch_shapes=[pltpu.VMEM((groups * local, LANES), jnp.float32)],
        compiler_params=pltpu.CompilerParams(vmem_limit_bytes=8 << 20),
        name="relax",
    )(field, weight)


def solution(mesh):
    placed = (P("sec", "tile", None, None, None), P("sec", None), P(None, "sec", "tile", None))
    return jax.shard_map(
        shards,
        mesh=mesh,
        in_specs=placed,
        out_specs=(P(None, "sec", "tile", None), P(None, "sec", None, "tile", None)),
        check_vma=False,
    )
```
